32 devices in a mesh: groups: 2 (over x), ctx: 16 (over z, y, core).
Axes of the slice: x: 2, y: 2, z: 4, core: 2. Of those that a mesh axis runs over, the one named last changes fastest.
Arguments:
- features: bfloat16 [4096, 3, 8192], P(('groups', 'ctx')), parts along dimension 0, may hold values from -6 to 6
- short_filter: bfloat16 [3, 3, 8192], P(None, None, 'ctx'), may hold values from -3.5 to 3.5
- residues: float32 [8192, 16], P('ctx'), may hold values from -1.5 to 1.5
- rates: float32 [8192, 16], P('ctx'), may hold values from 0.02 to 64
Outputs:
- gated: bfloat16 [4096, 8192], P(('groups', 'ctx')), parts along dimension 0
The draws below stay inside these ranges and needn't reach their ends.
There are 2 independent parts, one for each index of `groups`. The reference program is written for one: setup_inputs(seed, part) draws one part's arguments, and reference() takes and returns one part's arrays. A program takes and returns all parts, laid end to end along the dimension named above; an argument that names none is the same for every part. Nothing has to cross between parts.
All inputs are finite; a program needn't handle non-finite values.
Results may differ from the reference program's by a relative error of at most 0.001.
Values may be sent and summed in bfloat16 or wider, within the bound.
No kernel may reach another device: no remote copies, remote signals or barrier semaphores. Data moves between devices by JAX's collectives and lax.ppermute only.
A program may use at most 256 MiB of HBM per device.

```python
import math
import jax
import jax.numpy as jnp
from jax import lax

C = 8192
S = 16
BLOCK = 16
TOKENS = 2048
N_CTX = 16


def shard_levels(rng, dims, cuts, least, largest):
    loudness = 1.0
    for position, shards_of in cuts:
        heights = jax.random.uniform(jax.random.fold_in(jax.random.fold_in(rng, 6), position), (shards_of,), jnp.float32, least / len(cuts), largest / len(cuts))
        loudness = loudness * jnp.repeat(jnp.exp(heights), dims[position] // shards_of).reshape((-1,) + (1,) * (len(dims) - 1 - position))
    return loudness


def scatter_about(key, extent, scale, most, cuts=(), kind=jnp.bfloat16):
    drawn = scale * jax.random.normal(key, extent, jnp.float32)
    if cuts:
        drawn = drawn * shard_levels(key, extent, cuts, -0.22, 0.18)
    return jnp.clip(drawn, -most, most).astype(kind)


def setup_inputs(seed: int = 0, part: int = 0) -> dict:
    seeds = jax.random.split(jax.random.key(seed), 5)
    part_keys = jax.random.split(jax.random.fold_in(seeds[4], part), 5)
    return {
        "features": scatter_about(part_keys[0], (TOKENS, 3, C), 1.0, 6.0, ((0, 16),)),
        "short_filter": scatter_about(seeds[1], (3, 3, C), 3 ** -0.5, 3.5, ((2, 16),)),
        "residues": scatter_about(seeds[2], (C, S), 0.25, 1.5, ((0, 16),), jnp.float32),
        "rates": jnp.clip(jnp.exp(math.log(64.0) - 8.070906 * jax.random.uniform(seeds[3], (C, S), jnp.float32) ** shard_levels(seeds[3], (C, S), ((0, 16),), -0.2, 0.2)), 0.02, 64.0),
    }


def featurize(tail, feats, taps):
    full = jnp.concatenate([tail, feats], 0).astype(jnp.float32)
    rows = feats.shape[0]
    taps = taps.astype(jnp.float32)
    return taps[0] * full[2:] + taps[1] * full[1:rows + 1] + taps[2] * full[:rows]

def prepare(rates_t, coef_t, scale):
    lags = jnp.arange(BLOCK, dtype=jnp.float32)[:, None, None]
    powers = jnp.exp(-rates_t[None] * lags * scale)
    kernel = lax.optimization_barrier(jnp.sum(coef_t[None] * powers, axis=1))
    reach = coef_t[None] * powers * jnp.exp(-rates_t * scale)[None]
    block_decay = jnp.exp(-rates_t * (BLOCK * scale))
    return (powers, kernel, reach, block_decay)

def modal_local(drive, powers, kernel, block_decay):
    rows, width = drive.shape
    count = rows // BLOCK
    blocks = drive.reshape(count, BLOCK, width)
    intra = blocks * kernel[0]
    for lag in range(1, BLOCK):
        moved = jnp.pad(blocks[:, :BLOCK - lag], ((0, 0), (lag, 0), (0, 0)))
        intra = intra + kernel[lag] * moved
    ends = blocks[:, 0][:, None, :] * powers[BLOCK - 1][None]
    for place in range(1, BLOCK):
        ends = ends + blocks[:, place][:, None, :] * powers[BLOCK - 1 - place][None]

    def advance(carry, end):
        return (block_decay * carry + end, carry)
    local_end, starts = lax.scan(advance, jnp.zeros_like(block_decay), ends)
    return (intra, starts, local_end)

def modal_finish(intra, starts, reach, incoming, rates_t, scale):
    count = starts.shape[0]
    index = jnp.arange(count, dtype=jnp.float32)[:, None, None]
    starts = starts + jnp.exp(-rates_t[None] * (index * (BLOCK * scale))) * incoming[None]
    mixed = intra
    for mode in range(starts.shape[1]):
        mixed = mixed + starts[:, mode][:, None, :] * reach[:, mode][None]
    return mixed.reshape(-1, intra.shape[2])

def reference(features, short_filter, residues, rates):
    width = features.shape[2]
    rows = features.shape[0] // N_CTX
    scale = 1.0 / features.shape[0]
    rates_t = rates.T
    coef_t = (residues * jnp.sqrt(-jnp.expm1(-2.0 * rates * scale))).T
    powers, kernel, reach, block_decay = prepare(rates_t, coef_t, scale)
    shard_decay = jnp.exp(-rates_t * (rows * scale))
    shards = features.reshape(N_CTX, rows, 3, width)

    def step(carry, shard):
        tail, state = carry
        filtered = featurize(tail, shard, short_filter)
        drive = filtered[:, 1] * filtered[:, 2]
        intra, starts, local_end = modal_local(drive, powers, kernel, block_decay)
        mixed = modal_finish(intra, starts, reach, state, rates_t, scale)
        gated = (filtered[:, 0] * mixed).astype(jnp.bfloat16)
        new_state = local_end + shard_decay * state
        return ((shard[-2:], new_state), gated)
    init = (jnp.zeros((2, 3, width), jnp.bfloat16), jnp.zeros_like(rates_t))
    _, outs = lax.scan(step, init, shards)
    return outs.reshape(-1, width)
```

```python
import functools
import jax
import jax.numpy as jnp
from jax import lax
from jax.experimental import pallas as pl
from jax.experimental.pallas import tpu as pltpu
from jax.sharding import PartitionSpec as P

WIDTH = 512
LANES = 128
CHUNKS = WIDTH // LANES
HALF = 8
SUB = 8
TAPS = 9


def rows_out(scratch, natural, first, stride):
    for k in range(CHUNKS):
        scratch[pl.ds(first + k, natural.shape[0], stride=stride), :] = natural[
            :, k * LANES : (k + 1) * LANES
        ]


def modes_out(scratch, natural):
    for h in range(2):
        rows_out(scratch, natural[h * HALF : (h + 1) * HALF], h * CHUNKS, SUB)


def registers(scratch, count):
    return [scratch[j * SUB : (j + 1) * SUB, :] for j in range(count)]


def local_kernel(
    scale, unroll, ids, feats, tail, params, coef, ends, packed, fkv, fq, taps_s, a_s, c_s, s_s
):
    rows = feats.shape[1]
    rows_out(a_s, jnp.exp(params[0, 0:HALF] * (-scale)), 0, SUB)
    rows_out(a_s, jnp.exp(params[0, HALF : 2 * HALF] * (-scale)), CHUNKS, SUB)
    modes_out(c_s, coef[0])
    rows_out(taps_s, params[0, 2 * HALF : 2 * HALF + TAPS], CHUNKS, CHUNKS)
    for branch, dest, first in ((1, fkv, 0), (2, fkv, CHUNKS), (0, fq, CHUNKS)):
        rows_out(dest, tail[branch].astype(jnp.float32), first, SUB)
        rows_out(dest, feats[branch].astype(jnp.float32), 2 * SUB + first, SUB)
    a = registers(a_s, HALF)
    c = registers(c_s, HALF)
    tap = [taps_s[pl.ds(CHUNKS + (3 * j + 1) * CHUNKS, SUB), :] for j in range(3)]
    tap_q = [taps_s[pl.ds((3 * j) * CHUNKS, SUB), :] for j in range(3)]
    upper = lax.broadcasted_iota(jnp.int32, (SUB, LANES), 0) >= CHUNKS

    def step(t0, carry):
        state, f1, f2, q1, q2 = carry
        state = list(state)
        for u in range(unroll):
            at = pl.multiple_of((t0 * unroll + u + 2) * SUB, SUB)
            f0 = fkv[pl.ds(at, SUB), :]
            q0 = fq[pl.ds(at, SUB), :]
            filtered = tap[0] * f0 + tap[1] * f1 + tap[2] * f2
            query = tap_q[0] * q0 + tap_q[1] * q1 + tap_q[2] * q2
            drive = filtered * pltpu.roll(filtered, CHUNKS, 0)
            terms = []
            for j in range(HALF):
                state[j] = a[j] * state[j] + drive
                terms.append(c[j] * state[j])
            while len(terms) > 1:
                terms = [x + y for x, y in zip(terms[::2], terms[1::2])]
            y = terms[0] + pltpu.roll(terms[0], CHUNKS, 0)
            packed[0, pl.ds(pl.multiple_of((t0 * unroll + u) * SUB, SUB), SUB), :] = jnp.where(
                upper, query, y
            )
            f1, f2, q1, q2 = f0, f1, q0, q1
        return tuple(state), f1, f2, q1, q2

    zero = jnp.zeros((SUB, LANES), jnp.float32)
    start = (
        (zero,) * HALF,
        fkv[SUB : 2 * SUB, :],
        fkv[0:SUB, :],
        fq[SUB : 2 * SUB, :],
        fq[0:SUB, :],
    )
    state = lax.fori_loop(0, rows // unroll, step, start)[0]
    for j in range(HALF):
        s_s[j * SUB : (j + 1) * SUB, :] = state[j]
    for h in range(2):
        for k in range(CHUNKS):
            ends[0, h * HALF : (h + 1) * HALF, k * LANES : (k + 1) * LANES] = s_s[
                pl.ds(h * CHUNKS + k, HALF, stride=SUB), :
            ]


def finish_kernel(scale, unroll, ids, packed, params, coef, incoming, out, a_s, p_s, y_s):
    rows = out.shape[0]
    decay = jnp.exp(params[0, 0 : 2 * HALF] * (-scale))
    modes_out(a_s, decay)
    modes_out(p_s, coef[0] * decay * incoming[0])
    a = registers(a_s, HALF)

    def step(t0, p):
        p = list(p)
        for u in range(unroll):
            at = pl.multiple_of((t0 * unroll + u) * SUB, SUB)
            z = packed[0, pl.ds(at, SUB), :]
            terms = p
            while len(terms) > 1:
                terms = [x + y for x, y in zip(terms[::2], terms[1::2])]
            y = terms[0] + pltpu.roll(terms[0], CHUNKS, 0)
            y_s[pl.ds(at, SUB), :] = (z + y) * pltpu.roll(z, CHUNKS, 0)
            p = [x * d for x, d in zip(p, a)]
        return tuple(p)

    lax.fori_loop(0, rows // unroll, step, tuple(registers(p_s, HALF)))
    for k in range(CHUNKS):
        out[:, k * LANES : (k + 1) * LANES] = y_s[pl.ds(k, rows, stride=SUB), :].astype(out.dtype)


def by_piece(*shape):
    return pl.BlockSpec((1,) + shape, lambda i, ids: (i, 0, 0))


def local_part(ids, feats, tail, params, coef, scale):
    pieces, rows = params.shape[0], feats.shape[1]
    f32 = jnp.float32
    column = lambda i, ids: (0, 0, ids[i])
    return pl.pallas_call(
        functools.partial(local_kernel, scale, 8),
        out_shape=(
            jax.ShapeDtypeStruct((pieces, 2 * HALF, WIDTH), f32),
            jax.ShapeDtypeStruct((pieces, rows * SUB, LANES), f32),
        ),
        grid_spec=pltpu.PrefetchScalarGridSpec(
            num_scalar_prefetch=1,
            grid=(pieces,),
            in_specs=[
                pl.BlockSpec((3, rows, WIDTH), column),
                pl.BlockSpec((3, 2, WIDTH), column),
                by_piece(*params.shape[1:]),
                by_piece(*coef.shape[1:]),
            ],
            out_specs=[by_piece(2 * HALF, WIDTH), by_piece(rows * SUB, LANES)],
            scratch_shapes=[
                pltpu.VMEM(((rows + 2) * SUB, LANES), f32),
                pltpu.VMEM(((rows + 2) * SUB, LANES), f32),
                pltpu.VMEM(((TAPS + 1) * CHUNKS, LANES), f32),
                pltpu.VMEM((HALF * SUB, LANES), f32),
                pltpu.VMEM((HALF * SUB, LANES), f32),
                pltpu.VMEM((HALF * SUB, LANES), f32),
            ],
        ),
        name="local_part",
    )(ids, feats, tail, params, coef)


def finish_part(ids, packed, params, coef, incoming, scale):
    pieces, rows = packed.shape[0], packed.shape[1] // SUB
    f32 = jnp.float32
    return pl.pallas_call(
        functools.partial(finish_kernel, scale, 8),
        out_shape=jax.ShapeDtypeStruct((rows, pieces * WIDTH), jnp.bfloat16),
        grid_spec=pltpu.PrefetchScalarGridSpec(
            num_scalar_prefetch=1,
            grid=(pieces,),
            in_specs=[
                by_piece(rows * SUB, LANES),
                by_piece(*params.shape[1:]),
                by_piece(*coef.shape[1:]),
                by_piece(2 * HALF, WIDTH),
            ],
            out_specs=pl.BlockSpec((rows, WIDTH), lambda i, ids: (0, ids[i])),
            scratch_shapes=[
                pltpu.VMEM((HALF * SUB, LANES), f32),
                pltpu.VMEM((HALF * SUB, LANES), f32),
                pltpu.VMEM((rows * SUB, LANES), f32),
            ],
        ),
        name="finish_part",
    )(ids, packed, params, coef, incoming)


def swap(value, bit):
    size = lax.axis_size("ctx")
    return lax.ppermute(value, "ctx", [(i, i ^ bit) for i in range(size)])


def gather_pieces(value, bits):
    value = value[None]
    for bit in bits:
        value = jnp.concatenate([value, swap(value, bit)], 0)
    return value


def exchange_by_swaps(ends, rates, me, span, bits):
    split = bits[-2:]
    whole = bits[:-2]
    mine, kept, count = ends, [], 1
    decay = jnp.exp(rates * (-span))
    for bit in reversed(split):
        half = mine.shape[0] // 2
        theirs = swap(mine[half:], bit)
        mine, decay = mine[:half], decay[:half]
        later = (me & bit) != 0
        low = jnp.where(later, theirs, mine)
        high = jnp.where(later, mine, theirs)
        kept.append((bit, later, low, decay))
        mine = decay * low + high
        decay = decay * decay
    before = jnp.zeros_like(mine)
    total = mine
    reach = jnp.ones_like(decay)
    for bit in sorted(whole):
        place = whole.index(bit)
        flat = swap(total, bit)
        other = flat.reshape((2,) * len(whole) + flat.shape[1:])
        other = jnp.flip(other, len(whole) - 1 - place).reshape(flat.shape)
        later = (me & bit) != 0
        low = jnp.where(later, other, total)
        high = jnp.where(later, total, other)
        before = before + jnp.where(later, reach * low, 0.0)
        total = decay * low + high
        reach = reach * jnp.where(later, decay, 1.0)
        decay = decay * decay
    for bit, later, low, decay in reversed(kept):
        after = decay * before + low
        theirs = swap(jnp.where(later, before, after), bit)
        before = jnp.concatenate([jnp.where(later, after, before), theirs], 0)
    return before


def to_pieces(value):
    rows = value.shape[0]
    return value.reshape(rows, -1, WIDTH).transpose(1, 0, 2)


def exchange_by_owner(ends, rates_t, me, span):
    size = lax.axis_size("ctx")
    modes = ends.shape[1]
    blocks = ends.transpose(1, 0, 2).reshape(modes, size, -1).transpose(1, 0, 2)
    blocks = lax.all_to_all(blocks, "ctx", 0, 0, tiled=True)
    decay = jnp.exp(rates_t * (-span))

    def advance(carry, end):
        return decay * carry + end, carry

    before = lax.scan(advance, jnp.zeros_like(blocks[0]), blocks)[1]
    before = lax.all_to_all(before, "ctx", 0, 0, tiled=True)
    return to_pieces(before.transpose(1, 0, 2).reshape(modes, -1))


def per_device(features, short_filter, residues, rates):
    rows = features.shape[0]
    size = lax.axis_size("ctx")
    me = lax.axis_index("ctx")
    scale = 1.0 / (rows * size)
    feats = features.transpose(1, 0, 2)
    tail = lax.ppermute(feats[:, -2:], "ctx", [(i, i + 1) for i in range(size - 1)])
    rates_t = rates.T
    coef_t = (residues * jnp.sqrt(-jnp.expm1(-2.0 * rates * scale))).T
    taps = short_filter.astype(jnp.float32).reshape(TAPS, -1)
    params = jnp.concatenate([rates_t, taps], 0)
    by_swaps = rates.shape[0] == WIDTH and size == 16
    if by_swaps:
        bits = (8, 4, 2, 1)
        params_all = gather_pieces(params, bits)
        coef_all = gather_pieces(coef_t, bits)
        order = [0]
        for bit in bits:
            order += [x ^ bit for x in order]
        ids = jnp.bitwise_xor(jnp.array(order, jnp.int32), me.astype(jnp.int32))
    else:
        params_all = to_pieces(lax.all_gather(params, "ctx", axis=1, tiled=True))
        coef_all = to_pieces(lax.all_gather(coef_t, "ctx", axis=1, tiled=True))
        ids = jnp.arange(params_all.shape[0], dtype=jnp.int32)
    ends, packed = local_part(ids, feats, tail, params_all, coef_all, scale)
    if by_swaps:
        incoming = exchange_by_swaps(ends, params_all[:, : 2 * HALF], me, rows * scale, bits)
    else:
        incoming = exchange_by_owner(ends, rates_t, me, rows * scale)
    return finish_part(ids, packed, params_all, coef_all, incoming, scale)


def solution(mesh):
    in_specs = (
        P(("groups", "ctx"), None, None),
        P(None, None, "ctx"),
        P("ctx", None),
        P("ctx", None),
    )
    out_specs = P(("groups", "ctx"), None)
    return jax.shard_map(
        per_device, mesh=mesh, in_specs=in_specs, out_specs=out_specs, check_vma=False
    )
```

```python
import functools
import jax
import jax.numpy as jnp
from jax import lax
from jax.experimental import pallas as pl
from jax.experimental.pallas import tpu as pltpu
from jax.sharding import PartitionSpec as P

WIDTH = 512
LANES = 128
CHUNKS = WIDTH // LANES
HALF = 8
MODES = 2 * HALF
SUB = 8
TAPS = 9
RATE_COLS = 2 * WIDTH
TAP_COLS = RATE_COLS + WIDTH
PARAM_COLS = TAP_COLS + LANES
GROUP = 4
GROUPS = 4
UNROLL = 16
F32 = jnp.float32
VMEM = pl.BlockSpec(memory_space=pltpu.VMEM)


def rows_out(scratch, natural, first, stride):
    for k in range(CHUNKS):
        scratch[pl.ds(first + k, natural.shape[0], stride=stride), :] = natural[
            :, k * LANES : (k + 1) * LANES
        ]


def modes_out(scratch, natural):
    for h in range(2):
        rows_out(scratch, natural[h * HALF : (h + 1) * HALF], h * CHUNKS, SUB)


def rates_of(params, i):
    return jnp.concatenate([params[i, :, 0:WIDTH], params[i, :, WIDTH:RATE_COLS]], 0)


def taps_out(scratch, params, i, first, stride):
    rows_out(scratch, params[i, :, RATE_COLS:TAP_COLS], first, stride)
    at = first + stride * SUB
    scratch[at : at + CHUNKS, :] = params[i, 0:CHUNKS, TAP_COLS:PARAM_COLS]


def registers(scratch, count):
    return [scratch[j * SUB : (j + 1) * SUB, :] for j in range(count)]


def total(terms):
    while len(terms) > 1:
        terms = [x + y for x, y in zip(terms[::2], terms[1::2])]
    return terms[0]


def aligned(index):
    return pl.ds(pl.multiple_of(index, SUB), SUB)


def stage_body(branches, stride, feats, *refs):
    staged, done, held, sems = refs[-4:]
    rows, blocks = feats.shape[1], staged.shape[0]

    def fetch(i, b):
        column = pl.ds(i * WIDTH, WIDTH)
        return pltpu.make_async_copy(feats.at[branches[b], :, column], held.at[i, b], sems.at[i, b])

    for i in range(blocks):
        for b in range(len(branches)):
            fetch(i, b).start()
    for i in range(blocks):
        for b in range(len(branches)):
            fetch(i, b).wait()
            rows_out(staged.at[i], held[i, b].astype(F32), b * CHUNKS, stride)
    done[...] = jnp.zeros_like(done)


def pack_kernel(scale, filters, residues, rates, wide):
    for h in range(2):
        part = slice(h * HALF, (h + 1) * HALF)
        decayed = rates[part] * (2.0 * scale)
        power = jnp.tanh(0.5 * decayed) * (1.0 + jnp.exp(-decayed))
        wide[:, h * WIDTH : (h + 1) * WIDTH] = rates[part]
        at = PARAM_COLS + h * WIDTH
        wide[:, at : at + WIDTH] = residues[part] * jnp.sqrt(power)
    for r in range(TAPS):
        row = filters[r // 3, r % 3 : r % 3 + 1, :].astype(F32)
        if r < SUB:
            wide[r : r + 1, RATE_COLS:TAP_COLS] = row
        else:
            wide[:, TAP_COLS:PARAM_COLS] = jnp.zeros((SUB, LANES), F32)
            for k in range(CHUNKS):
                wide[k : k + 1, TAP_COLS:PARAM_COLS] = row[:, k * LANES : (k + 1) * LANES]


def stack_kernel(*refs):
    params, coef = refs[-2:]
    for i in range(GROUP):
        params[i] = refs[i][:, 0:PARAM_COLS]
        for h in range(2):
            at = PARAM_COLS + h * WIDTH
            coef[i, h * HALF : (h + 1) * HALF, :] = refs[i][:, at : at + WIDTH]


def ends_kernel(
    scale, group, i, me, keyed, tail, params, ends, drive, last_s, taps_s, a_s, s_s
):
    rows = drive.shape[1] // SUB
    block = me[0] ^ (GROUP * i + group)
    column = pl.ds(pl.multiple_of(block * WIDTH, WIDTH), WIDTH)
    modes_out(a_s, jnp.exp(rates_of(params, i) * (-scale)))
    taps_out(taps_s, params, i, 0, CHUNKS)
    for branch, first in ((1, 0), (2, CHUNKS)):
        rows_out(last_s, tail[branch, :, column].astype(F32), first, SUB)
    a = registers(a_s, HALF)
    tap = [taps_s[pl.ds((3 * j + 1) * CHUNKS, SUB), :] for j in range(3)]

    def step(t0, carry):
        state, f1, f2 = carry
        state = list(state)
        for u in range(UNROLL):
            at = aligned((t0 * UNROLL + u) * SUB)
            f0 = keyed[block, at, :]
            filtered = tap[0] * f0 + tap[1] * f1 + tap[2] * f2
            now = filtered * pltpu.roll(filtered, CHUNKS, 0)
            drive[i, at, :] = now
            for j in range(HALF):
                state[j] = a[j] * state[j] + now
            f1, f2 = f0, f1
        return tuple(state), f1, f2

    start = ((jnp.zeros((SUB, LANES), F32),) * HALF, last_s[SUB : 2 * SUB, :], last_s[0:SUB, :])
    state = lax.fori_loop(0, rows // UNROLL, step, start)[0]
    for j in range(HALF):
        s_s[j * SUB : (j + 1) * SUB, :] = state[j]
    for h in range(2):
        for k in range(CHUNKS):
            ends[i, h * HALF : (h + 1) * HALF, k * LANES : (k + 1) * LANES] = s_s[
                pl.ds(h * CHUNKS + k, HALF, stride=SUB), :
            ]


def inner_kernel(
    scale, group, i, me, query, tail, params, coef, drive, packed, last_s, taps_s, a_s, c_s
):
    rows = drive.shape[1] // SUB
    block = me[0] ^ (GROUP * i + group)
    column = pl.ds(pl.multiple_of(block * WIDTH, WIDTH), WIDTH)
    modes_out(a_s, jnp.exp(rates_of(params, i) * (-scale)))
    modes_out(c_s, coef[i])
    for twice in range(2):
        taps_out(taps_s, params, i, twice * CHUNKS, SUB)
    rows_out(last_s, tail[0, :, column].astype(F32), 0, CHUNKS)
    a = registers(a_s, HALF)
    c = registers(c_s, HALF)
    tap = [taps_s[3 * j * SUB : (3 * j + 1) * SUB, :] for j in range(3)]
    upper = lax.broadcasted_iota(jnp.int32, (SUB, LANES), 0) >= CHUNKS

    def step(t0, carry):
        state, before = carry
        state = list(state)
        for u in range(0, UNROLL, 2):
            latest = query[block, aligned((t0 * UNROLL + u) * CHUNKS), :]
            middle = pltpu.roll(jnp.where(upper, before, latest), CHUNKS, 0)
            filtered = tap[0] * latest + tap[1] * middle + tap[2] * before
            before = latest
            for v, q in ((0, pltpu.roll(filtered, CHUNKS, 0)), (1, filtered)):
                at = aligned((t0 * UNROLL + u + v) * SUB)
                now = drive[i, at, :]
                for j in range(HALF):
                    state[j] = a[j] * state[j] + now
                y = total([x * s for x, s in zip(c, state)])
                packed[i, at, :] = jnp.where(upper, q, y + pltpu.roll(y, CHUNKS, 0))
        return tuple(state), before

    start = ((jnp.zeros((SUB, LANES), F32),) * HALF, last_s[0:SUB, :])
    lax.fori_loop(0, rows // UNROLL, step, start)


def finish_kernel(scale, group, i, me, packed, params, coef, incoming, *refs):
    out, a_s, p_s, y_s, held, sems = refs[-6:]
    rows = out.shape[0]
    decay = jnp.exp(rates_of(params, i) * (-scale))
    modes_out(a_s, decay)
    modes_out(p_s, coef[i] * decay * incoming[i])
    a = registers(a_s, HALF)

    def step(t0, p):
        p = list(p)
        for u in range(UNROLL):
            at = aligned((t0 * UNROLL + u) * SUB)
            z = packed[i, at, :]
            y = total(p)
            y = y + pltpu.roll(y, CHUNKS, 0)
            y_s[at, :] = (z + y) * pltpu.roll(z, CHUNKS, 0)
            p = [x * d for x, d in zip(p, a)]
        return tuple(p)

    lax.fori_loop(0, rows // UNROLL, step, tuple(registers(p_s, HALF)))
    for k in range(CHUNKS):
        held[i, :, k * LANES : (k + 1) * LANES] = y_s[pl.ds(k, rows, stride=SUB), :].astype(
            out.dtype
        )
    columns_home(group, i, me, out, held, sems).start()


def columns_home(group, i, me, out, held, sems):
    column = pl.ds(pl.multiple_of((me[0] ^ (GROUP * i + group)) * WIDTH, WIDTH), WIDTH)
    return pltpu.make_async_copy(held.at[i], out.at[:, column], sems.at[i])


def pieces(kernel, last, skip, *refs):
    refs = refs[:1] + refs[1 + skip :]

    def one(i, carry):
        kernel(i, *refs)
        return carry

    lax.fori_loop(0, GROUP, one, 0)
    if last is not None:
        for i in range(GROUP):
            last(i, refs[0], refs[-6], refs[-2], refs[-1]).wait()


def whole(inputs, outputs, scratch, more=(), smem=1, room=4):
    return dict(
        compiler_params=pltpu.CompilerParams(vmem_limit_bytes=room << 20),
        in_specs=[pl.BlockSpec(memory_space=pltpu.SMEM)] * smem + inputs,
        out_specs=outputs,
        scratch_shapes=[pltpu.VMEM((n, LANES), F32) for n in scratch] + list(more),
    )


def cost(rows, ops):
    work = GROUP * rows * SUB * LANES * ops
    return pl.CostEstimate(flops=work, bytes_accessed=work // 4, transcendentals=0)


ANYWHERE = pl.BlockSpec(memory_space=pl.ANY)


def stage_part(branches, feats, *earlier):
    rows, blocks = feats.shape[1], feats.shape[2] // WIDTH
    stride = CHUNKS * len(branches)
    return pl.pallas_call(
        functools.partial(stage_body, branches, stride),
        out_shape=(
            pltpu.VMEM((blocks, rows * stride, LANES), F32),
            pltpu.VMEM((SUB, LANES), F32),
        ),
        cost_estimate=cost(rows, 20 * len(branches)),
        name="stage_part",
        **whole(
            [pl.BlockSpec(memory_space=pltpu.HBM)] + [ANYWHERE] * len(earlier),
            [VMEM] * 2,
            (),
            (
                pltpu.VMEM((blocks, len(branches), rows, WIDTH), feats.dtype),
                pltpu.SemaphoreType.DMA((blocks, len(branches))),
            ),
            smem=0,
            room=8,
        ),
    )(feats, *earlier)


def pack_part(filters, residues, rates, scale):
    return pl.pallas_call(
        functools.partial(pack_kernel, scale),
        out_shape=pltpu.VMEM((SUB, PARAM_COLS + 2 * WIDTH), F32),
        grid=(1,),
        name="pack_part",
        compiler_params=pltpu.CompilerParams(vmem_limit_bytes=4 << 20),
    )(filters, residues, rates)


def stack_part(parts, *earlier):
    return pl.pallas_call(
        stack_kernel,
        out_shape=(
            pltpu.VMEM((GROUP, SUB, PARAM_COLS), F32),
            pltpu.VMEM((GROUP, MODES, WIDTH), F32),
        ),
        cost_estimate=pl.CostEstimate(flops=1 << 18, bytes_accessed=1 << 18, transcendentals=0),
        name="stack_part",
        **whole([VMEM] * GROUP + [ANYWHERE] * len(earlier), [VMEM] * 2, (), smem=0),
    )(*parts, *earlier)


def ends_part(group, me, keyed, tail, params, scale, *earlier):
    rows = keyed.shape[1] // SUB
    return pl.pallas_call(
        functools.partial(
            pieces, functools.partial(ends_kernel, scale, group), None, len(earlier)
        ),
        out_shape=(
            pltpu.VMEM((GROUP, MODES, WIDTH), F32),
            pltpu.VMEM((GROUP, rows * SUB, LANES), F32),
        ),
        cost_estimate=cost(rows, 24),
        name="ends_part",
        **whole(
            [ANYWHERE] * len(earlier) + [VMEM] * 3,
            [VMEM] * 2,
            (2 * SUB, TAPS * CHUNKS, HALF * SUB, HALF * SUB),
        ),
    )(me, *earlier, keyed, tail, params)


def inner_part(group, me, query, tail, params, coef, drive, scale):
    rows = drive.shape[1] // SUB
    return pl.pallas_call(
        functools.partial(pieces, functools.partial(inner_kernel, scale, group), None, 0),
        out_shape=pltpu.VMEM((GROUP, rows * SUB, LANES), F32),
        cost_estimate=cost(rows, 36),
        name="inner_part",
        **whole([VMEM] * 5, VMEM, (2 * CHUNKS, TAPS * SUB, HALF * SUB, HALF * SUB)),
    )(me, query, tail, params, coef, drive)


def finish_part(group, me, packed, params, coef, incoming, out, scale):
    rows = packed.shape[1] // SUB
    given = [] if out is None else [out]
    return pl.pallas_call(
        functools.partial(
            pieces,
            functools.partial(finish_kernel, scale, group),
            functools.partial(columns_home, group),
            0,
        ),
        out_shape=jax.ShapeDtypeStruct((rows, GROUPS * GROUP * WIDTH), jnp.bfloat16),
        cost_estimate=cost(rows, 20),
        name="finish_part",
        input_output_aliases={5: 0} if given else {},
        **whole(
            [VMEM] * 4 + [pl.BlockSpec(memory_space=pl.ANY)] * len(given),
            pl.BlockSpec(memory_space=pl.ANY),
            (HALF * SUB, HALF * SUB, rows * SUB),
            (
                pltpu.VMEM((GROUP, rows, WIDTH), jnp.bfloat16),
                pltpu.SemaphoreType.DMA((GROUP,)),
            ),
        ),
    )(me, packed, params, coef, incoming, *given)


CORE, Y, Z = 1, 2, 4


def swap(value, bit):
    size = lax.axis_size("ctx")
    return lax.ppermute(value, "ctx", [(i, i ^ bit) for i in range(size)])


def small(kernel, count, name, me, *args):
    return pl.pallas_call(
        kernel,
        out_shape=tuple(pltpu.VMEM((GROUP, MODES, WIDTH), F32) for _ in range(count)),
        cost_estimate=pl.CostEstimate(flops=1 << 18, bytes_accessed=1 << 18, transcendentals=0),
        name=name,
        **whole([VMEM] * len(args), [VMEM] * count, ()),
    )(me, *args)


def join_kernel(bit, span, flip, me, mine, theirs, params, low, both):
    later = (me[0] & bit) != 0
    for i in range(GROUP):
        m, t = mine[i], theirs[i ^ flip]
        decay = jnp.exp(rates_of(params, i) * (-span))
        first = jnp.where(later, t, m)
        low[i] = first
        both[i] = decay * first + jnp.where(later, m, t)


def turn_kernel(span, me, first, far, plane_low, core_low, params, row_out, mine, core_out):
    core, row = (me[0] & CORE) != 0, (me[0] & Y) != 0
    odd, high = (me[0] & Z) != 0, (me[0] & (2 * Z)) != 0
    for i in range(GROUP):
        rates = rates_of(params, i)
        reach = jnp.where(odd, jnp.exp(rates * (-4 * span)), 1.0)
        before = jnp.where(odd, first[i], 0.0) + jnp.where(high, reach * far[i ^ 2], 0.0)
        after = jnp.exp(rates * (-2 * span)) * before + plane_low[i]
        row_out[i] = jnp.where(row, before, after)
        before = jnp.where(row, after, before)
        after = jnp.exp(rates * (-span)) * before + core_low[i]
        core_out[i] = jnp.where(core, before, after)
        mine[i] = jnp.where(core, after, before)


def core_kernel(span, me, given, core_low, params, mine, core_out):
    core = (me[0] & CORE) != 0
    for i in range(GROUP):
        before = given[i]
        after = jnp.exp(rates_of(params, i) * (-span)) * before + core_low[i]
        core_out[i] = jnp.where(core, before, after)
        mine[i] = jnp.where(core, after, before)


def join(bit, span, flip, *args):
    return small(functools.partial(join_kernel, bit, span, flip), 2, "join", *args)


def after(value, *others):
    return lax.optimization_barrier((value,) + others)


def to_groups(value):
    pieces = value.reshape(value.shape[0], -1, WIDTH).transpose(1, 0, 2)
    return [pieces[g::GROUPS] for g in range(GROUPS)]


def by_owner(ends, rates_t, span):
    size = lax.axis_size("ctx")
    pieces = jnp.stack(ends, 1).reshape((-1,) + ends[0].shape[1:])
    blocks = pieces.transpose(1, 0, 2).reshape(MODES, size, -1).transpose(1, 0, 2)
    blocks = lax.all_to_all(blocks, "ctx", 0, 0, tiled=True)
    decay = jnp.exp(rates_t * (-span))

    def advance(carry, end):
        return decay * carry + end, carry

    before = lax.scan(advance, jnp.zeros_like(blocks[0]), blocks)[1]
    before = lax.all_to_all(before, "ctx", 0, 0, tiled=True)
    return to_groups(before.transpose(1, 0, 2).reshape(MODES, -1))


def by_gathers(feats, tail, short_filter, residues, rates, scale, span):
    rates_t = rates.T
    taps = short_filter.astype(F32).reshape(TAPS, -1)
    coef_t = (residues * jnp.sqrt(-jnp.expm1(-2.0 * rates * scale))).T
    named = jnp.concatenate([rates_t, taps, coef_t], 0)
    named = lax.all_gather(named, "ctx", axis=1, tiled=True)
    last = named[MODES + SUB].reshape(-1, CHUNKS, LANES)
    last = jnp.pad(last, ((0, 0), (0, SUB - CHUNKS), (0, 0)))
    named = named.reshape(named.shape[0], -1, WIDTH).transpose(1, 0, 2)
    parts = [named[:, k * SUB : (k + 1) * SUB] for k in range(3)]
    params = jnp.concatenate(parts + [last], 2)
    params = [params[g::GROUPS] for g in range(GROUPS)]
    coef = [named[g::GROUPS, MODES + TAPS :] for g in range(GROUPS)]
    base = jnp.zeros((1,), jnp.int32)
    keyed, query = stage_part((1, 2), feats)[0], stage_part((0,), feats)[0]
    groups = range(GROUPS)
    ends, drive = zip(*[ends_part(g, base, keyed, tail, params[g], scale) for g in groups])
    packed = [inner_part(g, base, query, tail, params[g], coef[g], drive[g], scale) for g in groups]
    incoming = by_owner(ends, rates_t, span)
    out = None
    for g in groups:
        out = finish_part(g, base, packed[g], params[g], coef[g], incoming[g], out, scale)
    return out


def per_device(features, short_filter, residues, rates):
    rows = features.shape[0]
    size = lax.axis_size("ctx")
    me = lax.axis_index("ctx").astype(jnp.int32)
    scale = 1.0 / (rows * size)
    feats = features.transpose(1, 0, 2)
    tail_rows = feats[:, -2:]
    tail = lax.ppermute(tail_rows, "ctx", [(i, i + 1) for i in range(size - 1)])
    rates_t = rates.T
    span = rows * scale
    swaps = rates.shape[0] == WIDTH and size == GROUP * GROUPS
    if not swaps:
        return by_gathers(feats, tail, short_filter, residues, rates, scale, span)

    base = me.reshape(1)
    wide = pack_part(short_filter, residues.T, rates_t, scale)
    near = [swap(wide, Z * k) for k in range(1, GROUP)]
    keyed, staged = stage_part((1, 2), feats, tail_rows, base)
    params, coef = ([x] for x in stack_part([wide] + near, staged, tail))
    params.append(swap(params[0], CORE))
    params.append(swap(params[0], Y))
    coef.append(swap(coef[0], CORE))
    query, staged = stage_part((0,), feats, params[0])
    ends, drive, packed = [None] * GROUPS, [None] * GROUPS, [None] * GROUPS

    def run_ends(g, *earlier):
        ends[g], drive[g] = ends_part(g, base, keyed, tail, params[g], scale, *earlier)

    def run_inner(g):
        packed[g] = inner_part(g, base, query, tail, params[g], coef[g], drive[g], scale)

    run_ends(1)
    from_1 = swap(ends[1], CORE)
    run_ends(0)
    params[2], ends[0], from_1, _ = after(params[2], ends[0], from_1, staged)
    params.append(swap(params[2], CORE))
    run_ends(2)
    low_z, chip_z = join(CORE, span, 0, base, ends[0], from_1, params[0])
    params[3], ends[2], chip_z = after(params[3], ends[2], chip_z)
    run_ends(3)
    from_3 = swap(ends[3], CORE)
    low_y, chip_y = join(CORE, span, 0, base, ends[2], from_3, params[2])
    from_y = swap(chip_y, Y)
    run_inner(0)
    from_y, packed[0], drive[1] = after(from_y, packed[0], drive[1])
    low, plane = join(Y, 2 * span, 0, base, chip_z, from_y, params[0])
    from_near = swap(plane, Z)
    coef.append(swap(coef[0], Y))
    run_inner(1)
    from_near, packed[1], coef[2] = after(from_near, packed[1], coef[2])
    first, pair = join(Z, 4 * span, 1, base, plane, from_near, params[0])
    from_far = swap(pair, 2 * Z)
    coef.append(swap(coef[2], CORE))
    run_inner(2)
    run_inner(3)
    from_far, packed[2], packed[3] = after(from_far, packed[2], packed[3])
    to_row, mine_z, to_core = small(
        functools.partial(turn_kernel, span),
        3,
        "turn",
        base,
        first,
        from_far,
        low,
        low_z,
        params[0],
    )
    from_row = swap(to_row, Y)
    core_z = swap(to_core, CORE)
    out = finish_part(0, base, packed[0], params[0], coef[0], mine_z, None, scale)
    out = finish_part(1, base, packed[1], params[1], coef[1], core_z, out, scale)
    from_row, out = after(from_row, out)
    mine_y, to_core = small(
        functools.partial(core_kernel, span), 2, "turn_core", base, from_row, low_y, params[2]
    )
    core_y = swap(to_core, CORE)
    out = finish_part(2, base, packed[2], params[2], coef[2], mine_y, out, scale)
    return finish_part(3, base, packed[3], params[3], coef[3], core_y, out, scale)


def solution(mesh):
    in_specs = (
        P(("groups", "ctx"), None, None),
        P(None, None, "ctx"),
        P("ctx", None),
        P("ctx", None),
    )
    out_specs = P(("groups", "ctx"), None)
    return jax.shard_map(
        per_device, mesh=mesh, in_specs=in_specs, out_specs=out_specs, check_vma=False
    )
```

```python
import functools
import jax
import jax.numpy as jnp
from jax import lax
from jax.experimental import pallas as pl
from jax.experimental.pallas import tpu as pltpu
from jax.sharding import PartitionSpec as P

WIDTH = 512
LANES = 128
CHUNKS = WIDTH // LANES
HALF = 8
MODES = 2 * HALF
SUB = 8
TAPS = 9
RATE_COLS = 2 * WIDTH
TAP_COLS = RATE_COLS + WIDTH
PARAM_COLS = TAP_COLS + LANES
GROUP = 4
GROUPS = 4
UNROLL = 32
HBM = pl.BlockSpec(memory_space=pltpu.HBM)
F32 = jnp.float32
VMEM = pl.BlockSpec(memory_space=pltpu.VMEM)


def rows_out(scratch, natural, first, stride):
    for k in range(CHUNKS):
        scratch[pl.ds(first + k, natural.shape[0], stride=stride), :] = natural[
            :, k * LANES : (k + 1) * LANES
        ]


def modes_out(scratch, natural):
    for h in range(2):
        rows_out(scratch, natural[h * HALF : (h + 1) * HALF], h * CHUNKS, SUB)


def rates_of(params, i):
    return jnp.concatenate([params[i, :, 0:WIDTH], params[i, :, WIDTH:RATE_COLS]], 0)


def taps_out(scratch, params, i, first, stride):
    rows_out(scratch, params[i, :, RATE_COLS:TAP_COLS], first, stride)
    at = first + stride * SUB
    scratch[at : at + CHUNKS, :] = params[i, 0:CHUNKS, TAP_COLS:PARAM_COLS]


def registers(scratch, count):
    return [scratch[j * SUB : (j + 1) * SUB, :] for j in range(count)]


def total(terms):
    while len(terms) > 1:
        terms = [x + y for x, y in zip(terms[::2], terms[1::2])]
    return terms[0]


def aligned(index):
    return pl.ds(pl.multiple_of(index, SUB), SUB)


def stage_body(branches, stride, feats, *refs):
    staged, done, held, sems = refs[-4:]
    rows, blocks = feats.shape[1], staged.shape[0]

    def fetch(i, b):
        column = pl.ds(i * WIDTH, WIDTH)
        return pltpu.make_async_copy(feats.at[branches[b], :, column], held.at[i, b], sems.at[i, b])

    for i in range(blocks):
        for b in range(len(branches)):
            fetch(i, b).start()
    for i in range(blocks):
        for b in range(len(branches)):
            fetch(i, b).wait()
            rows_out(staged.at[i], held[i, b].astype(F32), b * CHUNKS, stride)
    done[...] = jnp.zeros_like(done)


def pack_kernel(scale, filters_in, residues_in, rates_in, wide, filters, residues, rates, sems):
    copies = [
        pltpu.make_async_copy(source, dest, sems.at[n])
        for n, (source, dest) in enumerate(
            ((rates_in, rates), (residues_in, residues), (filters_in, filters))
        )
    ]
    for copy in copies:
        copy.start()
    copies[0].wait()
    copies[1].wait()
    for h in range(2):
        part = slice(h * HALF, (h + 1) * HALF)
        decayed = rates[part, :] * (2.0 * scale)
        power = jnp.tanh(0.5 * decayed) * (1.0 + jnp.exp(-decayed))
        wide[:, h * WIDTH : (h + 1) * WIDTH] = rates[part, :]
        at = PARAM_COLS + h * WIDTH
        wide[:, at : at + WIDTH] = residues[part, :] * jnp.sqrt(power)
    copies[2].wait()
    wide[:, TAP_COLS:PARAM_COLS] = jnp.zeros((SUB, LANES), F32)
    for r in range(TAPS):
        row = filters[r // 3, r % 3 : r % 3 + 1, :].astype(F32)
        if r < SUB:
            wide[r : r + 1, RATE_COLS:TAP_COLS] = row
        else:
            for k in range(CHUNKS):
                wide[k : k + 1, TAP_COLS:PARAM_COLS] = row[:, k * LANES : (k + 1) * LANES]


def tail_kernel(feats, *refs):
    tail, last, sem = refs[-3:]
    rows = feats.shape[1]
    copy = pltpu.make_async_copy(feats.at[:, rows - SUB : rows, :], last, sem)
    copy.start()
    copy.wait()
    for b in range(3):
        tail[b] = last[b, SUB - 2 : SUB, :]


def stack_kernel(*refs):
    params, coef = refs[-2:]
    for i in range(GROUP):
        params[i] = refs[i][:, 0:PARAM_COLS]
        for h in range(2):
            at = PARAM_COLS + h * WIDTH
            coef[i, h * HALF : (h + 1) * HALF, :] = refs[i][:, at : at + WIDTH]


def ends_kernel(
    scale, group, i, me, keyed, tail, params, ends, drive, last_s, taps_s, a_s, s_s
):
    rows = drive.shape[1] // SUB
    block = me[0] ^ (GROUP * i + group)
    column = pl.ds(pl.multiple_of(block * WIDTH, WIDTH), WIDTH)
    modes_out(a_s, jnp.exp(rates_of(params, i) * (-scale)))
    taps_out(taps_s, params, i, 0, CHUNKS)
    for branch, first in ((1, 0), (2, CHUNKS)):
        rows_out(last_s, tail[branch, :, column].astype(F32), first, SUB)
    a = registers(a_s, HALF)
    tap = [taps_s[pl.ds((3 * j + 1) * CHUNKS, SUB), :] for j in range(3)]

    def step(t0, carry):
        state, f1, f2 = carry
        state = list(state)
        for u in range(UNROLL):
            at = aligned((t0 * UNROLL + u) * SUB)
            f0 = keyed[block, at, :]
            filtered = tap[0] * f0 + tap[1] * f1 + tap[2] * f2
            now = filtered * pltpu.roll(filtered, CHUNKS, 0)
            drive[i, at, :] = now
            for j in range(HALF):
                state[j] = a[j] * state[j] + now
            f1, f2 = f0, f1
        return tuple(state), f1, f2

    start = ((jnp.zeros((SUB, LANES), F32),) * HALF, last_s[SUB : 2 * SUB, :], last_s[0:SUB, :])
    state = lax.fori_loop(0, rows // UNROLL, step, start)[0]
    for j in range(HALF):
        s_s[j * SUB : (j + 1) * SUB, :] = state[j]
    for h in range(2):
        for k in range(CHUNKS):
            ends[i, h * HALF : (h + 1) * HALF, k * LANES : (k + 1) * LANES] = s_s[
                pl.ds(h * CHUNKS + k, HALF, stride=SUB), :
            ]


def inner_kernel(
    scale, group, i, me, query, tail, params, coef, drive, packed, last_s, taps_s, a_s, c_s
):
    rows = drive.shape[1] // SUB
    block = me[0] ^ (GROUP * i + group)
    column = pl.ds(pl.multiple_of(block * WIDTH, WIDTH), WIDTH)
    modes_out(a_s, jnp.exp(rates_of(params, i) * (-scale)))
    modes_out(c_s, coef[i])
    for twice in range(2):
        taps_out(taps_s, params, i, twice * CHUNKS, SUB)
    rows_out(last_s, tail[0, :, column].astype(F32), 0, CHUNKS)
    a = registers(a_s, HALF)
    c = registers(c_s, HALF)
    tap = [taps_s[3 * j * SUB : (3 * j + 1) * SUB, :] for j in range(3)]
    upper = lax.broadcasted_iota(jnp.int32, (SUB, LANES), 0) >= CHUNKS

    def step(t0, carry):
        state, before = carry
        state = list(state)
        for u in range(0, UNROLL, 2):
            latest = query[block, aligned((t0 * UNROLL + u) * CHUNKS), :]
            middle = pltpu.roll(jnp.where(upper, before, latest), CHUNKS, 0)
            filtered = tap[0] * latest + tap[1] * middle + tap[2] * before
            before = latest
            for v, q in ((0, pltpu.roll(filtered, CHUNKS, 0)), (1, filtered)):
                at = aligned((t0 * UNROLL + u + v) * SUB)
                now = drive[i, at, :]
                for j in range(HALF):
                    state[j] = a[j] * state[j] + now
                y = total([x * s for x, s in zip(c, state)])
                packed[i, at, :] = jnp.where(upper, q, y + pltpu.roll(y, CHUNKS, 0))
        return tuple(state), before

    start = ((jnp.zeros((SUB, LANES), F32),) * HALF, last_s[0:SUB, :])
    lax.fori_loop(0, rows // UNROLL, step, start)


def finish_kernel(scale, i, params, packed, coef, incoming, held, a_s, p_s, y_s):
    rows = held.shape[1]
    decay = jnp.exp(rates_of(params, i) * (-scale))
    modes_out(a_s, decay)
    modes_out(p_s, coef[i] * decay * incoming[i])
    a = registers(a_s, HALF)

    def step(t0, p):
        p = list(p)
        for u in range(UNROLL):
            at = aligned((t0 * UNROLL + u) * SUB)
            z = packed[i, at, :]
            y = total(p)
            y = y + pltpu.roll(y, CHUNKS, 0)
            y_s[at, :] = (z + y) * pltpu.roll(z, CHUNKS, 0)
            p = [x * d for x, d in zip(p, a)]
        return tuple(p)

    lax.fori_loop(0, rows // UNROLL, step, tuple(registers(p_s, HALF)))
    for k in range(CHUNKS):
        held[i, :, k * LANES : (k + 1) * LANES] = y_s[pl.ds(k, rows, stride=SUB), :].astype(
            held.dtype
        )


def finish_body(scale, group, me, packed, params, coef, incoming, *refs):
    final = group == GROUPS - 1
    mine, a_s, p_s, y_s, sems = refs[-5:]
    out = refs[-6] if group else None

    def home(source, g, i, sem):
        column = pl.ds(pl.multiple_of((me[0] ^ (GROUP * i + g)) * WIDTH, WIDTH), WIDTH)
        return pltpu.make_async_copy(source.at[i], out.at[:, column], sems.at[sem, i])

    if group:
        for i in range(GROUP):
            home(refs[0], group - 1, i, 0).start()

    def one(i, carry):
        finish_kernel(scale, i, params, packed, coef, incoming, mine, a_s, p_s, y_s)
        if final:
            home(mine, group, i, 1).start()
        return carry

    lax.fori_loop(0, GROUP, one, 0)
    for i in range(GROUP):
        if group:
            home(refs[0], group - 1, i, 0).wait()
        if final:
            home(mine, group, i, 1).wait()


def pieces(kernel, skip, *refs):
    refs = refs[:1] + refs[1 + skip :]

    def one(i, carry):
        kernel(i, *refs)
        return carry

    lax.fori_loop(0, GROUP, one, 0)


def whole(inputs, outputs, scratch, more=(), smem=1, room=4):
    return dict(
        compiler_params=pltpu.CompilerParams(vmem_limit_bytes=room << 20),
        in_specs=[pl.BlockSpec(memory_space=pltpu.SMEM)] * smem + inputs,
        out_specs=outputs,
        scratch_shapes=[pltpu.VMEM((n, LANES), F32) for n in scratch] + list(more),
    )


def cost(rows, ops):
    work = GROUP * rows * SUB * LANES * ops
    return pl.CostEstimate(flops=work, bytes_accessed=work // 4, transcendentals=0)


ANYWHERE = pl.BlockSpec(memory_space=pl.ANY)


def stage_part(branches, feats, *earlier):
    rows, blocks = feats.shape[1], feats.shape[2] // WIDTH
    stride = CHUNKS * len(branches)
    return pl.pallas_call(
        functools.partial(stage_body, branches, stride),
        out_shape=(
            pltpu.VMEM((blocks, rows * stride, LANES), F32),
            pltpu.VMEM((SUB, LANES), F32),
        ),
        cost_estimate=cost(rows, 20 * len(branches)),
        name="stage_part",
        **whole(
            [HBM] + [ANYWHERE] * len(earlier),
            [VMEM] * 2,
            (),
            (
                pltpu.VMEM((blocks, len(branches), rows, WIDTH), feats.dtype),
                pltpu.SemaphoreType.DMA((blocks, len(branches))),
            ),
            smem=0,
            room=8,
        ),
    )(in_hbm(feats), *earlier)


def in_hbm(value):
    return pltpu.with_memory_space_constraint(value, pltpu.HBM)


def pack_part(filters, residues, rates, scale):
    return pl.pallas_call(
        functools.partial(pack_kernel, scale),
        out_shape=pltpu.VMEM((SUB, PARAM_COLS + 2 * WIDTH), F32),
        name="pack_part",
        **whole(
            [HBM] * 3,
            VMEM,
            (),
            (
                pltpu.VMEM(filters.shape, filters.dtype),
                pltpu.VMEM((MODES, WIDTH), F32),
                pltpu.VMEM((MODES, WIDTH), F32),
                pltpu.SemaphoreType.DMA((3,)),
            ),
            smem=0,
        ),
    )(in_hbm(filters), in_hbm(residues), in_hbm(rates))


def tail_part(feats, *earlier):
    width = feats.shape[2]
    return pl.pallas_call(
        tail_kernel,
        out_shape=pltpu.VMEM((3, 2, width), feats.dtype),
        name="tail_part",
        **whole(
            [HBM] + [ANYWHERE] * len(earlier),
            VMEM,
            (),
            (pltpu.VMEM((3, SUB, width), feats.dtype), pltpu.SemaphoreType.DMA),
            smem=0,
        ),
    )(in_hbm(feats), *earlier)


def stack_part(parts, *earlier):
    return pl.pallas_call(
        stack_kernel,
        out_shape=(
            pltpu.VMEM((GROUP, SUB, PARAM_COLS), F32),
            pltpu.VMEM((GROUP, MODES, WIDTH), F32),
        ),
        cost_estimate=pl.CostEstimate(flops=1 << 18, bytes_accessed=1 << 18, transcendentals=0),
        name="stack_part",
        **whole([VMEM] * GROUP + [ANYWHERE] * len(earlier), [VMEM] * 2, (), smem=0),
    )(*parts, *earlier)


def ends_part(group, me, keyed, tail, params, scale, *earlier):
    rows = keyed.shape[1] // SUB
    return pl.pallas_call(
        functools.partial(
            pieces, functools.partial(ends_kernel, scale, group), len(earlier)
        ),
        out_shape=(
            pltpu.VMEM((GROUP, MODES, WIDTH), F32),
            pltpu.VMEM((GROUP, rows * SUB, LANES), F32),
        ),
        cost_estimate=cost(rows, 24),
        name="ends_part",
        **whole(
            [ANYWHERE] * len(earlier) + [VMEM] * 3,
            [VMEM] * 2,
            (2 * SUB, TAPS * CHUNKS, HALF * SUB, HALF * SUB),
        ),
    )(me, *earlier, keyed, tail, params)


def inner_part(group, me, query, tail, params, coef, drive, scale):
    rows = drive.shape[1] // SUB
    return pl.pallas_call(
        functools.partial(pieces, functools.partial(inner_kernel, scale, group), 0),
        out_shape=pltpu.VMEM((GROUP, rows * SUB, LANES), F32),
        cost_estimate=cost(rows, 36),
        name="inner_part",
        **whole([VMEM] * 5, VMEM, (2 * CHUNKS, TAPS * SUB, HALF * SUB, HALF * SUB)),
    )(me, query, tail, params, coef, drive)


def finish_part(group, me, packed, params, coef, incoming, before, scale):
    rows, width = packed.shape[1] // SUB, GROUPS * GROUP * WIDTH
    final = group == GROUPS - 1
    held = (GROUP, rows, WIDTH)
    out_shape, out_specs, more = [], [], []
    if group:
        out_shape.append(jax.ShapeDtypeStruct((rows, width), jnp.bfloat16))
        out_specs.append(ANYWHERE)
    if final:
        more.append(pltpu.VMEM(held, jnp.bfloat16))
    else:
        out_shape.append(pltpu.VMEM(held, jnp.bfloat16))
        out_specs.append(VMEM)
    given_specs = [VMEM, ANYWHERE][: len(before)]
    spec = whole(
        [VMEM] * 4 + given_specs,
        out_specs,
        (),
        more
        + [pltpu.VMEM((n, LANES), F32) for n in (HALF * SUB, HALF * SUB, rows * SUB)]
        + [pltpu.SemaphoreType.DMA((2, GROUP))],
    )
    return pl.pallas_call(
        functools.partial(finish_body, scale, group),
        out_shape=out_shape,
        cost_estimate=cost(rows, 20),
        name="finish_part",
        input_output_aliases={6: 0} if len(before) > 1 else {},
        **spec,
    )(me, packed, params, coef, incoming, *before)


CORE, Y, Z = 1, 2, 4


def swap(value, bit):
    size = lax.axis_size("ctx")
    return lax.ppermute(value, "ctx", [(i, i ^ bit) for i in range(size)])


def small(kernel, count, name, me, *args):
    return pl.pallas_call(
        kernel,
        out_shape=tuple(pltpu.VMEM((GROUP, MODES, WIDTH), F32) for _ in range(count)),
        cost_estimate=pl.CostEstimate(flops=1 << 18, bytes_accessed=1 << 18, transcendentals=0),
        name=name,
        **whole([VMEM] * len(args), [VMEM] * count, ()),
    )(me, *args)


def join_kernel(bit, span, flip, me, mine, theirs, params, low, both):
    later = (me[0] & bit) != 0
    for i in range(GROUP):
        m, t = mine[i], theirs[i ^ flip]
        decay = jnp.exp(rates_of(params, i) * (-span))
        first = jnp.where(later, t, m)
        low[i] = first
        both[i] = decay * first + jnp.where(later, m, t)


def turn_kernel(span, me, first, far, plane_low, core_low, params, row_out, mine, core_out):
    core, row = (me[0] & CORE) != 0, (me[0] & Y) != 0
    odd, high = (me[0] & Z) != 0, (me[0] & (2 * Z)) != 0
    for i in range(GROUP):
        rates = rates_of(params, i)
        reach = jnp.where(odd, jnp.exp(rates * (-4 * span)), 1.0)
        before = jnp.where(odd, first[i], 0.0) + jnp.where(high, reach * far[i ^ 2], 0.0)
        after = jnp.exp(rates * (-2 * span)) * before + plane_low[i]
        row_out[i] = jnp.where(row, before, after)
        before = jnp.where(row, after, before)
        after = jnp.exp(rates * (-span)) * before + core_low[i]
        core_out[i] = jnp.where(core, before, after)
        mine[i] = jnp.where(core, after, before)


def core_kernel(span, me, given, core_low, params, mine, core_out):
    core = (me[0] & CORE) != 0
    for i in range(GROUP):
        before = given[i]
        after = jnp.exp(rates_of(params, i) * (-span)) * before + core_low[i]
        core_out[i] = jnp.where(core, before, after)
        mine[i] = jnp.where(core, after, before)


def join(bit, span, flip, *args):
    return small(functools.partial(join_kernel, bit, span, flip), 2, "join", *args)


def after(value, *others):
    return lax.optimization_barrier((value,) + others)


def to_groups(value):
    pieces = value.reshape(value.shape[0], -1, WIDTH).transpose(1, 0, 2)
    return [pieces[g::GROUPS] for g in range(GROUPS)]


def by_owner(ends, rates_t, span):
    size = lax.axis_size("ctx")
    pieces = jnp.stack(ends, 1).reshape((-1,) + ends[0].shape[1:])
    blocks = pieces.transpose(1, 0, 2).reshape(MODES, size, -1).transpose(1, 0, 2)
    blocks = lax.all_to_all(blocks, "ctx", 0, 0, tiled=True)
    decay = jnp.exp(rates_t * (-span))

    def advance(carry, end):
        return decay * carry + end, carry

    before = lax.scan(advance, jnp.zeros_like(blocks[0]), blocks)[1]
    before = lax.all_to_all(before, "ctx", 0, 0, tiled=True)
    return to_groups(before.transpose(1, 0, 2).reshape(MODES, -1))


def by_gathers(feats, tail, short_filter, residues, rates, scale, span):
    rates_t = rates.T
    taps = short_filter.astype(F32).reshape(TAPS, -1)
    coef_t = (residues * jnp.sqrt(-jnp.expm1(-2.0 * rates * scale))).T
    named = jnp.concatenate([rates_t, taps, coef_t], 0)
    named = lax.all_gather(named, "ctx", axis=1, tiled=True)
    last = named[MODES + SUB].reshape(-1, CHUNKS, LANES)
    last = jnp.pad(last, ((0, 0), (0, SUB - CHUNKS), (0, 0)))
    named = named.reshape(named.shape[0], -1, WIDTH).transpose(1, 0, 2)
    parts = [named[:, k * SUB : (k + 1) * SUB] for k in range(3)]
    params = jnp.concatenate(parts + [last], 2)
    params = [params[g::GROUPS] for g in range(GROUPS)]
    coef = [named[g::GROUPS, MODES + TAPS :] for g in range(GROUPS)]
    base = jnp.zeros((1,), jnp.int32)
    keyed, query = stage_part((1, 2), feats)[0], stage_part((0,), feats)[0]
    groups = range(GROUPS)
    ends, drive = zip(*[ends_part(g, base, keyed, tail, params[g], scale) for g in groups])
    packed = [inner_part(g, base, query, tail, params[g], coef[g], drive[g], scale) for g in groups]
    incoming = by_owner(ends, rates_t, span)
    done = ()
    for g in groups:
        done = finish_part(g, base, packed[g], params[g], coef[g], incoming[g], done[::-1], scale)
    return done[0]


def per_device(features, short_filter, residues, rates):
    rows = features.shape[0]
    size = lax.axis_size("ctx")
    me = lax.axis_index("ctx").astype(jnp.int32)
    scale = 1.0 / (rows * size)
    feats = features.transpose(1, 0, 2)
    onward = [(i, i + 1) for i in range(size - 1)]
    span = rows * scale
    if rates.shape[0] != WIDTH or size != GROUP * GROUPS:
        tail = lax.ppermute(feats[:, -2:], "ctx", onward)
        return by_gathers(feats, tail, short_filter, residues, rates, scale, span)

    base = me.reshape(1)
    wide = pack_part(short_filter, residues.T, rates.T, scale)
    near = [swap(wide, Z * k) for k in range(1, GROUP)]
    keyed, staged = stage_part((1, 2), feats, wide, base)
    tail_rows = tail_part(feats, staged)
    params, coef = ([x] for x in stack_part([wide] + near, tail_rows))
    params.append(swap(params[0], CORE))
    params.append(swap(params[0], Y))
    query, staged = stage_part((0,), feats, params[0])
    tail = lax.ppermute(tail_rows, "ctx", onward)
    coef.append(swap(coef[0], CORE))
    ends, drive, packed = [None] * GROUPS, [None] * GROUPS, [None] * GROUPS

    def run_ends(g, *earlier):
        ends[g], drive[g] = ends_part(g, base, keyed, tail, params[g], scale, *earlier)

    def run_inner(g):
        packed[g] = inner_part(g, base, query, tail, params[g], coef[g], drive[g], scale)

    run_ends(1, staged)
    from_1 = swap(ends[1], CORE)
    run_ends(0)
    params[2], ends[0], from_1 = after(params[2], ends[0], from_1)
    params.append(swap(params[2], CORE))
    run_ends(2)
    low_z, chip_z = join(CORE, span, 0, base, ends[0], from_1, params[0])
    params[3], ends[2], chip_z = after(params[3], ends[2], chip_z)
    run_ends(3)
    from_3 = swap(ends[3], CORE)
    low_y, chip_y = join(CORE, span, 0, base, ends[2], from_3, params[2])
    from_y = swap(chip_y, Y)
    run_inner(0)
    from_y, packed[0], drive[1] = after(from_y, packed[0], drive[1])
    low, plane = join(Y, 2 * span, 0, base, chip_z, from_y, params[0])
    from_near = swap(plane, Z)
    coef.append(swap(coef[0], Y))
    run_inner(1)
    from_near, packed[1], coef[2] = after(from_near, packed[1], coef[2])
    first, pair = join(Z, 4 * span, 1, base, plane, from_near, params[0])
    from_far = swap(pair, 2 * Z)
    coef.append(swap(coef[2], CORE))
    run_inner(2)
    run_inner(3)
    from_far, packed[2], packed[3] = after(from_far, packed[2], packed[3])
    to_row, mine_z, to_core = small(
        functools.partial(turn_kernel, span),
        3,
        "turn",
        base,
        first,
        from_far,
        low,
        low_z,
        params[0],
    )
    from_row = swap(to_row, Y)
    core_z = swap(to_core, CORE)
    done = finish_part(0, base, packed[0], params[0], coef[0], mine_z, (), scale)
    done = finish_part(1, base, packed[1], params[1], coef[1], core_z, done[::-1], scale)
    from_row, held = after(from_row, done[1])
    mine_y, to_core = small(
        functools.partial(core_kernel, span), 2, "turn_core", base, from_row, low_y, params[2]
    )
    core_y = swap(to_core, CORE)
    done = finish_part(2, base, packed[2], params[2], coef[2], mine_y, (held, done[0]), scale)
    return finish_part(3, base, packed[3], params[3], coef[3], core_y, done[::-1], scale)[0]


def solution(mesh):
    in_specs = (
        P(("groups", "ctx"), None, None),
        P(None, None, "ctx"),
        P("ctx", None),
        P("ctx", None),
    )
    out_specs = P(("groups", "ctx"), None)
    return jax.shard_map(
        per_device, mesh=mesh, in_specs=in_specs, out_specs=out_specs, check_vma=False
    )
```

```python
import functools
import jax
import jax.numpy as jnp
from jax import lax
from jax.experimental import pallas as pl
from jax.experimental.pallas import tpu as pltpu
from jax.sharding import PartitionSpec as P

WIDTH = 512
LANES = 128
CHUNKS = WIDTH // LANES
HALF = 8
MODES = 2 * HALF
SUB = 8
TAPS = 9
RATE_COLS = 2 * WIDTH
TAP_COLS = RATE_COLS + WIDTH
PARAM_COLS = TAP_COLS + LANES
GROUP = 4
GROUPS = 4
UNROLL = 64
HBM = pl.BlockSpec(memory_space=pltpu.HBM)
F32 = jnp.float32
VMEM = pl.BlockSpec(memory_space=pltpu.VMEM)


def rows_out(scratch, natural, first, stride):
    for k in range(CHUNKS):
        scratch[pl.ds(first + k, natural.shape[0], stride=stride), :] = natural[
            :, k * LANES : (k + 1) * LANES
        ]


def modes_out(scratch, natural):
    for h in range(2):
        rows_out(scratch, natural[h * HALF : (h + 1) * HALF], h * CHUNKS, SUB)


def rates_of(params, i):
    return jnp.concatenate([params[i, :, 0:WIDTH], params[i, :, WIDTH:RATE_COLS]], 0)


def taps_out(scratch, params, i, first, stride):
    rows_out(scratch, params[i, :, RATE_COLS:TAP_COLS], first, stride)
    at = first + stride * SUB
    scratch[at : at + CHUNKS, :] = params[i, 0:CHUNKS, TAP_COLS:PARAM_COLS]


def registers(scratch, count):
    return [scratch[j * SUB : (j + 1) * SUB, :] for j in range(count)]


def total(terms):
    while len(terms) > 1:
        terms = [x + y for x, y in zip(terms[::2], terms[1::2])]
    return terms[0]


def aligned(index):
    return pl.ds(pl.multiple_of(index, SUB), SUB)


def stage_body(branches, stride, feats, *refs):
    staged, done, held, sems = refs[-4:]
    rows, blocks = feats.shape[1], staged.shape[0]

    def fetch(i, b):
        column = pl.ds(i * WIDTH, WIDTH)
        return pltpu.make_async_copy(feats.at[branches[b], :, column], held.at[i, b], sems.at[i, b])

    for i in range(blocks):
        for b in range(len(branches)):
            fetch(i, b).start()
    for i in range(blocks):
        for b in range(len(branches)):
            fetch(i, b).wait()
            rows_out(staged.at[i], held[i, b].astype(F32), b * CHUNKS, stride)
    done[...] = jnp.zeros_like(done)


def pack_kernel(
    scale, filters_in, residues_in, rates_in, feats, wide, tail, filters, residues, rates, last, sems
):
    count = feats.shape[1]
    copies = [
        pltpu.make_async_copy(source, dest, sems.at[n])
        for n, (source, dest) in enumerate(
            (
                (rates_in, rates),
                (residues_in, residues),
                (filters_in, filters),
                (feats.at[:, count - SUB : count, :], last),
            )
        )
    ]
    for copy in copies:
        copy.start()
    copies[0].wait()
    copies[1].wait()
    for h in range(2):
        part = slice(h * HALF, (h + 1) * HALF)
        decayed = rates[part, :] * (2.0 * scale)
        power = jnp.tanh(0.5 * decayed) * (1.0 + jnp.exp(-decayed))
        wide[:, h * WIDTH : (h + 1) * WIDTH] = rates[part, :]
        at = PARAM_COLS + h * WIDTH
        wide[:, at : at + WIDTH] = residues[part, :] * jnp.sqrt(power)
    copies[2].wait()
    wide[:, TAP_COLS:PARAM_COLS] = jnp.zeros((SUB, LANES), F32)
    for r in range(TAPS):
        row = filters[r // 3, r % 3 : r % 3 + 1, :].astype(F32)
        if r < SUB:
            wide[r : r + 1, RATE_COLS:TAP_COLS] = row
        else:
            for k in range(CHUNKS):
                wide[k : k + 1, TAP_COLS:PARAM_COLS] = row[:, k * LANES : (k + 1) * LANES]
    copies[3].wait()
    for b in range(3):
        tail[b] = last[b, SUB - 2 : SUB, :]


def stack_kernel(*refs):
    params, coef = refs[-2:]
    for ref, i in zip(refs, NEAR + (0,)):
        params[i] = ref[:, 0:PARAM_COLS]
        for h in range(2):
            at = PARAM_COLS + h * WIDTH
            coef[i, h * HALF : (h + 1) * HALF, :] = ref[:, at : at + WIDTH]


def ends_kernel(
    scale, group, i, me, keyed, tail, params, ends, drive, last_s, taps_s, a_s, s_s
):
    rows = drive.shape[1] // SUB
    block = me[0] ^ (GROUP * i + group)
    column = pl.ds(pl.multiple_of(block * WIDTH, WIDTH), WIDTH)
    modes_out(a_s, jnp.exp(rates_of(params, i) * (-scale)))
    taps_out(taps_s, params, i, 0, CHUNKS)
    for branch, first in ((1, 0), (2, CHUNKS)):
        rows_out(last_s, tail[branch, :, column].astype(F32), first, SUB)
    a = registers(a_s, HALF)
    tap = [taps_s[pl.ds((3 * j + 1) * CHUNKS, SUB), :] for j in range(3)]

    def step(t0, carry):
        state, f1, f2 = carry
        state = list(state)
        for u in range(UNROLL):
            at = aligned((t0 * UNROLL + u) * SUB)
            f0 = keyed[block, at, :]
            filtered = tap[0] * f0 + tap[1] * f1 + tap[2] * f2
            now = filtered * pltpu.roll(filtered, CHUNKS, 0)
            drive[i, at, :] = now
            for j in range(HALF):
                state[j] = a[j] * state[j] + now
            f1, f2 = f0, f1
        return tuple(state), f1, f2

    start = ((jnp.zeros((SUB, LANES), F32),) * HALF, last_s[SUB : 2 * SUB, :], last_s[0:SUB, :])
    state = lax.fori_loop(0, rows // UNROLL, step, start)[0]
    for j in range(HALF):
        s_s[j * SUB : (j + 1) * SUB, :] = state[j]
    for h in range(2):
        for k in range(CHUNKS):
            ends[i, h * HALF : (h + 1) * HALF, k * LANES : (k + 1) * LANES] = s_s[
                pl.ds(h * CHUNKS + k, HALF, stride=SUB), :
            ]


def inner_kernel(
    scale, group, i, me, query, tail, params, coef, drive, packed, last_s, taps_s, a_s, c_s
):
    rows = drive.shape[1] // SUB
    block = me[0] ^ (GROUP * i + group)
    column = pl.ds(pl.multiple_of(block * WIDTH, WIDTH), WIDTH)
    modes_out(a_s, jnp.exp(rates_of(params, i) * (-scale)))
    modes_out(c_s, coef[i])
    for twice in range(2):
        taps_out(taps_s, params, i, twice * CHUNKS, SUB)
    rows_out(last_s, tail[0, :, column].astype(F32), 0, CHUNKS)
    a = registers(a_s, HALF)
    c = registers(c_s, HALF)
    tap = [taps_s[3 * j * SUB : (3 * j + 1) * SUB, :] for j in range(3)]
    upper = lax.broadcasted_iota(jnp.int32, (SUB, LANES), 0) >= CHUNKS

    def step(t0, carry):
        state, before = carry
        state = list(state)
        for u in range(0, UNROLL, 2):
            latest = query[block, aligned((t0 * UNROLL + u) * CHUNKS), :]
            middle = pltpu.roll(jnp.where(upper, before, latest), CHUNKS, 0)
            filtered = tap[0] * latest + tap[1] * middle + tap[2] * before
            before = latest
            for v, q in ((0, pltpu.roll(filtered, CHUNKS, 0)), (1, filtered)):
                at = aligned((t0 * UNROLL + u + v) * SUB)
                now = drive[i, at, :]
                for j in range(HALF):
                    state[j] = a[j] * state[j] + now
                y = total([x * s for x, s in zip(c, state)])
                packed[i, at, :] = jnp.where(upper, q, y + pltpu.roll(y, CHUNKS, 0))
        return tuple(state), before

    start = ((jnp.zeros((SUB, LANES), F32),) * HALF, last_s[0:SUB, :])
    lax.fori_loop(0, rows // UNROLL, step, start)


def finish_kernel(scale, i, params, packed, coef, incoming, held, a_s, p_s, y_s):
    rows = held.shape[1]
    decay = jnp.exp(rates_of(params, i) * (-scale))
    modes_out(a_s, decay)
    modes_out(p_s, coef[i] * decay * incoming[i])
    a = registers(a_s, HALF)

    def step(t0, p):
        p = list(p)
        for u in range(UNROLL):
            at = aligned((t0 * UNROLL + u) * SUB)
            z = packed[i, at, :]
            y = total(p)
            y = y + pltpu.roll(y, CHUNKS, 0)
            y_s[at, :] = (z + y) * pltpu.roll(z, CHUNKS, 0)
            p = [x * d for x, d in zip(p, a)]
        return tuple(p)

    lax.fori_loop(0, rows // UNROLL, step, tuple(registers(p_s, HALF)))
    for k in range(CHUNKS):
        held[i, :, k * LANES : (k + 1) * LANES] = y_s[pl.ds(k, rows, stride=SUB), :].astype(
            held.dtype
        )


def finish_body(scale, group, me, packed, params, coef, incoming, *refs):
    final = group == GROUPS - 1
    mine, a_s, p_s, y_s, sems = refs[-5:]
    out = refs[-6] if group else None

    def home(source, g, i, sem):
        column = pl.ds(pl.multiple_of((me[0] ^ (GROUP * i + g)) * WIDTH, WIDTH), WIDTH)
        return pltpu.make_async_copy(source.at[i], out.at[:, column], sems.at[sem, i])

    if group:
        for i in range(GROUP):
            home(refs[0], group - 1, i, 0).start()

    def one(i, carry):
        finish_kernel(scale, i, params, packed, coef, incoming, mine, a_s, p_s, y_s)
        if final:
            home(mine, group, i, 1).start()
        return carry

    lax.fori_loop(0, GROUP, one, 0)
    for i in range(GROUP):
        if group:
            home(refs[0], group - 1, i, 0).wait()
        if final:
            home(mine, group, i, 1).wait()


def pieces(kernel, skip, *refs):
    refs = refs[:1] + refs[1 + skip :]

    def one(i, carry):
        kernel(i, *refs)
        return carry

    lax.fori_loop(0, GROUP, one, 0)


def whole(inputs, outputs, scratch, more=(), smem=1, room=4):
    return dict(
        compiler_params=pltpu.CompilerParams(vmem_limit_bytes=room << 20),
        in_specs=[pl.BlockSpec(memory_space=pltpu.SMEM)] * smem + inputs,
        out_specs=outputs,
        scratch_shapes=[pltpu.VMEM((n, LANES), F32) for n in scratch] + list(more),
    )


def cost(rows, ops):
    work = GROUP * rows * SUB * LANES * ops
    return pl.CostEstimate(flops=work, bytes_accessed=work // 4, transcendentals=0)


ANYWHERE = pl.BlockSpec(memory_space=pl.ANY)


def stage_part(branches, feats, *earlier):
    rows, blocks = feats.shape[1], feats.shape[2] // WIDTH
    stride = CHUNKS * len(branches)
    return pl.pallas_call(
        functools.partial(stage_body, branches, stride),
        out_shape=(
            pltpu.VMEM((blocks, rows * stride, LANES), F32),
            pltpu.VMEM((SUB, LANES), F32),
        ),
        cost_estimate=cost(rows, 20 * len(branches)),
        name="stage_part",
        **whole(
            [HBM] + [ANYWHERE] * len(earlier),
            [VMEM] * 2,
            (),
            (
                pltpu.VMEM((blocks, len(branches), rows, WIDTH), feats.dtype),
                pltpu.SemaphoreType.DMA((blocks, len(branches))),
            ),
            smem=0,
            room=8,
        ),
    )(in_hbm(feats), *earlier)


def in_hbm(value):
    return pltpu.with_memory_space_constraint(value, pltpu.HBM)


def pack_part(filters, residues, rates, feats, scale):
    width = feats.shape[2]
    return pl.pallas_call(
        functools.partial(pack_kernel, scale),
        out_shape=(
            pltpu.VMEM((SUB, PARAM_COLS + 2 * WIDTH), F32),
            pltpu.VMEM((3, 2, width), feats.dtype),
        ),
        name="pack_part",
        **whole(
            [HBM] * 4,
            [VMEM] * 2,
            (),
            (
                pltpu.VMEM(filters.shape, filters.dtype),
                pltpu.VMEM((MODES, WIDTH), F32),
                pltpu.VMEM((MODES, WIDTH), F32),
                pltpu.VMEM((3, SUB, width), feats.dtype),
                pltpu.SemaphoreType.DMA((4,)),
            ),
            smem=0,
        ),
    )(in_hbm(filters), in_hbm(residues), in_hbm(rates), in_hbm(feats))


def stack_part(parts, *earlier):
    return pl.pallas_call(
        stack_kernel,
        out_shape=(
            pltpu.VMEM((GROUP, SUB, PARAM_COLS), F32),
            pltpu.VMEM((GROUP, MODES, WIDTH), F32),
        ),
        cost_estimate=pl.CostEstimate(flops=1 << 18, bytes_accessed=1 << 18, transcendentals=0),
        name="stack_part",
        **whole([VMEM] * GROUP + [ANYWHERE] * len(earlier), [VMEM] * 2, (), smem=0),
    )(*parts, *earlier)


def ends_part(group, me, keyed, tail, params, scale, *earlier):
    rows = keyed.shape[1] // SUB
    return pl.pallas_call(
        functools.partial(
            pieces, functools.partial(ends_kernel, scale, group), len(earlier)
        ),
        out_shape=(
            pltpu.VMEM((GROUP, MODES, WIDTH), F32),
            pltpu.VMEM((GROUP, rows * SUB, LANES), F32),
        ),
        cost_estimate=cost(rows, 24),
        name="ends_part",
        **whole(
            [ANYWHERE] * len(earlier) + [VMEM] * 3,
            [VMEM] * 2,
            (2 * SUB, TAPS * CHUNKS, HALF * SUB, HALF * SUB),
        ),
    )(me, *earlier, keyed, tail, params)


def inner_part(group, me, query, tail, params, coef, drive, scale):
    rows = drive.shape[1] // SUB
    return pl.pallas_call(
        functools.partial(pieces, functools.partial(inner_kernel, scale, group), 0),
        out_shape=pltpu.VMEM((GROUP, rows * SUB, LANES), F32),
        cost_estimate=cost(rows, 36),
        name="inner_part",
        **whole([VMEM] * 5, VMEM, (2 * CHUNKS, TAPS * SUB, HALF * SUB, HALF * SUB)),
    )(me, query, tail, params, coef, drive)


def finish_part(group, me, packed, params, coef, incoming, before, scale):
    rows, width = packed.shape[1] // SUB, GROUPS * GROUP * WIDTH
    final = group == GROUPS - 1
    held = (GROUP, rows, WIDTH)
    out_shape, out_specs, more = [], [], []
    if group:
        out_shape.append(jax.ShapeDtypeStruct((rows, width), jnp.bfloat16))
        out_specs.append(ANYWHERE)
    if final:
        more.append(pltpu.VMEM(held, jnp.bfloat16))
    else:
        out_shape.append(pltpu.VMEM(held, jnp.bfloat16))
        out_specs.append(VMEM)
    given_specs = [VMEM, ANYWHERE][: len(before)]
    spec = whole(
        [VMEM] * 4 + given_specs,
        out_specs,
        (),
        more
        + [pltpu.VMEM((n, LANES), F32) for n in (HALF * SUB, HALF * SUB, rows * SUB)]
        + [pltpu.SemaphoreType.DMA((2, GROUP))],
    )
    return pl.pallas_call(
        functools.partial(finish_body, scale, group),
        out_shape=out_shape,
        cost_estimate=cost(rows, 20),
        name="finish_part",
        input_output_aliases={6: 0} if len(before) > 1 else {},
        **spec,
    )(me, packed, params, coef, incoming, *before)


CORE, Y, Z = 1, 2, 4
NEAR = (3, 2, 1)


def swap(value, bit):
    size = lax.axis_size("ctx")
    return lax.ppermute(value, "ctx", [(i, i ^ bit) for i in range(size)])


def small(kernel, count, name, me, *args):
    return pl.pallas_call(
        kernel,
        out_shape=tuple(pltpu.VMEM((GROUP, MODES, WIDTH), F32) for _ in range(count)),
        cost_estimate=pl.CostEstimate(flops=1 << 18, bytes_accessed=1 << 18, transcendentals=0),
        name=name,
        **whole([VMEM] * len(args), [VMEM] * count, ()),
    )(me, *args)


def join_kernel(bit, span, flip, me, mine, theirs, params, low, both):
    later = (me[0] & bit) != 0
    for i in range(GROUP):
        m, t = mine[i], theirs[i ^ flip]
        decay = jnp.exp(rates_of(params, i) * (-span))
        first = jnp.where(later, t, m)
        low[i] = first
        both[i] = decay * first + jnp.where(later, m, t)


def turn_kernel(span, me, first, far, plane_low, core_low, params, row_out, mine, core_out):
    core, row = (me[0] & CORE) != 0, (me[0] & Y) != 0
    odd, high = (me[0] & Z) != 0, (me[0] & (2 * Z)) != 0
    for i in range(GROUP):
        rates = rates_of(params, i)
        reach = jnp.where(odd, jnp.exp(rates * (-4 * span)), 1.0)
        before = jnp.where(odd, first[i], 0.0) + jnp.where(high, reach * far[i ^ 2], 0.0)
        after = jnp.exp(rates * (-2 * span)) * before + plane_low[i]
        row_out[i] = jnp.where(row, before, after)
        before = jnp.where(row, after, before)
        after = jnp.exp(rates * (-span)) * before + core_low[i]
        core_out[i] = jnp.where(core, before, after)
        mine[i] = jnp.where(core, after, before)


def core_kernel(span, me, given, core_low, params, mine, core_out):
    core = (me[0] & CORE) != 0
    for i in range(GROUP):
        before = given[i]
        after = jnp.exp(rates_of(params, i) * (-span)) * before + core_low[i]
        core_out[i] = jnp.where(core, before, after)
        mine[i] = jnp.where(core, after, before)


def join(bit, span, flip, *args):
    return small(functools.partial(join_kernel, bit, span, flip), 2, "join", *args)


def after(value, *others):
    return lax.optimization_barrier((value,) + others)


def to_groups(value):
    pieces = value.reshape(value.shape[0], -1, WIDTH).transpose(1, 0, 2)
    return [pieces[g::GROUPS] for g in range(GROUPS)]


def by_owner(ends, rates_t, span):
    size = lax.axis_size("ctx")
    pieces = jnp.stack(ends, 1).reshape((-1,) + ends[0].shape[1:])
    blocks = pieces.transpose(1, 0, 2).reshape(MODES, size, -1).transpose(1, 0, 2)
    blocks = lax.all_to_all(blocks, "ctx", 0, 0, tiled=True)
    decay = jnp.exp(rates_t * (-span))

    def advance(carry, end):
        return decay * carry + end, carry

    before = lax.scan(advance, jnp.zeros_like(blocks[0]), blocks)[1]
    before = lax.all_to_all(before, "ctx", 0, 0, tiled=True)
    return to_groups(before.transpose(1, 0, 2).reshape(MODES, -1))


def by_gathers(feats, tail, short_filter, residues, rates, scale, span):
    rates_t = rates.T
    taps = short_filter.astype(F32).reshape(TAPS, -1)
    coef_t = (residues * jnp.sqrt(-jnp.expm1(-2.0 * rates * scale))).T
    named = jnp.concatenate([rates_t, taps, coef_t], 0)
    named = lax.all_gather(named, "ctx", axis=1, tiled=True)
    last = named[MODES + SUB].reshape(-1, CHUNKS, LANES)
    last = jnp.pad(last, ((0, 0), (0, SUB - CHUNKS), (0, 0)))
    named = named.reshape(named.shape[0], -1, WIDTH).transpose(1, 0, 2)
    parts = [named[:, k * SUB : (k + 1) * SUB] for k in range(3)]
    params = jnp.concatenate(parts + [last], 2)
    params = [params[g::GROUPS] for g in range(GROUPS)]
    coef = [named[g::GROUPS, MODES + TAPS :] for g in range(GROUPS)]
    base = jnp.zeros((1,), jnp.int32)
    keyed, query = stage_part((1, 2), feats)[0], stage_part((0,), feats)[0]
    groups = range(GROUPS)
    ends, drive = zip(*[ends_part(g, base, keyed, tail, params[g], scale) for g in groups])
    packed = [inner_part(g, base, query, tail, params[g], coef[g], drive[g], scale) for g in groups]
    incoming = by_owner(ends, rates_t, span)
    done = ()
    for g in groups:
        done = finish_part(g, base, packed[g], params[g], coef[g], incoming[g], done[::-1], scale)
    return done[0]


def per_device(features, short_filter, residues, rates):
    rows = features.shape[0]
    size = lax.axis_size("ctx")
    me = lax.axis_index("ctx").astype(jnp.int32)
    scale = 1.0 / (rows * size)
    feats = features.transpose(1, 0, 2)
    onward = [(i, i + 1) for i in range(size - 1)]
    span = rows * scale
    if rates.shape[0] != WIDTH or size != GROUP * GROUPS:
        tail = lax.ppermute(feats[:, -2:], "ctx", onward)
        return by_gathers(feats, tail, short_filter, residues, rates, scale, span)

    base = me.reshape(1)
    wide, tail_rows = pack_part(short_filter, residues.T, rates.T, feats, scale)
    near = [swap(wide, Z * k) for k in NEAR]
    tail = lax.ppermute(tail_rows, "ctx", onward)
    keyed, staged = stage_part((1, 2), feats, wide, base)
    query, staged = stage_part((0,), feats, staged)
    params, coef = ([x] for x in stack_part(near + [wide], staged, tail))
    params.append(swap(params[0], CORE))
    params.append(swap(params[0], Y))
    tail = lax.ppermute(tail_rows, "ctx", onward)
    coef.append(swap(coef[0], CORE))
    ends, drive, packed = [None] * GROUPS, [None] * GROUPS, [None] * GROUPS

    def run_ends(g, *earlier):
        ends[g], drive[g] = ends_part(g, base, keyed, tail, params[g], scale, *earlier)

    def run_inner(g):
        packed[g] = inner_part(g, base, query, tail, params[g], coef[g], drive[g], scale)

    run_ends(1)
    from_1 = swap(ends[1], CORE)
    run_ends(0)
    params[2], ends[0], from_1 = after(params[2], ends[0], from_1)
    params.append(swap(params[2], CORE))
    run_ends(2)
    low_z, chip_z = join(CORE, span, 0, base, ends[0], from_1, params[0])
    params[3], ends[2], chip_z = after(params[3], ends[2], chip_z)
    run_ends(3)
    from_3 = swap(ends[3], CORE)
    low_y, chip_y = join(CORE, span, 0, base, ends[2], from_3, params[2])
    from_y = swap(chip_y, Y)
    run_inner(0)
    from_y, packed[0], drive[1] = after(from_y, packed[0], drive[1])
    low, plane = join(Y, 2 * span, 0, base, chip_z, from_y, params[0])
    from_near = swap(plane, Z)
    coef.append(swap(coef[0], Y))
    run_inner(1)
    from_near, packed[1], coef[2] = after(from_near, packed[1], coef[2])
    first, pair = join(Z, 4 * span, 1, base, plane, from_near, params[0])
    from_far = swap(pair, 2 * Z)
    coef.append(swap(coef[2], CORE))
    run_inner(2)
    run_inner(3)
    from_far, packed[2], packed[3] = after(from_far, packed[2], packed[3])
    to_row, mine_z, to_core = small(
        functools.partial(turn_kernel, span),
        3,
        "turn",
        base,
        first,
        from_far,
        low,
        low_z,
        params[0],
    )
    from_row = swap(to_row, Y)
    core_z = swap(to_core, CORE)
    done = finish_part(0, base, packed[0], params[0], coef[0], mine_z, (), scale)
    done = finish_part(1, base, packed[1], params[1], coef[1], core_z, done[::-1], scale)
    from_row, held = after(from_row, done[1])
    mine_y, to_core = small(
        functools.partial(core_kernel, span), 2, "turn_core", base, from_row, low_y, params[2]
    )
    core_y = swap(to_core, CORE)
    done = finish_part(2, base, packed[2], params[2], coef[2], mine_y, (held, done[0]), scale)
    return finish_part(3, base, packed[3], params[3], coef[3], core_y, done[::-1], scale)[0]


def solution(mesh):
    in_specs = (
        P(("groups", "ctx"), None, None),
        P(None, None, "ctx"),
        P("ctx", None),
        P("ctx", None),
    )
    out_specs = P(("groups", "ctx"), None)
    return jax.shard_map(
        per_device, mesh=mesh, in_specs=in_specs, out_specs=out_specs, check_vma=False
    )
```

```python
import functools
import jax
import jax.numpy as jnp
from jax import lax
from jax.experimental import pallas as pl
from jax.experimental.pallas import tpu as pltpu
from jax.sharding import PartitionSpec as P

WIDTH = 512
LANES = 128
CHUNKS = WIDTH // LANES
HALF = 8
MODES = 2 * HALF
SUB = 8
TAPS = 9
RATE_COLS = 2 * WIDTH
TAP_COLS = RATE_COLS + WIDTH
PARAM_COLS = TAP_COLS + LANES
GROUP = 4
GROUPS = 4
UNROLL = 128
HBM = pl.BlockSpec(memory_space=pltpu.HBM)
F32 = jnp.float32
VMEM = pl.BlockSpec(memory_space=pltpu.VMEM)


def rows_out(scratch, natural, first, stride):
    for k in range(CHUNKS):
        scratch[pl.ds(first + k, natural.shape[0], stride=stride), :] = natural[
            :, k * LANES : (k + 1) * LANES
        ]


def modes_out(scratch, natural):
    for h in range(2):
        rows_out(scratch, natural[h * HALF : (h + 1) * HALF], h * CHUNKS, SUB)


def rates_of(params, i):
    return jnp.concatenate([params[i, :, 0:WIDTH], params[i, :, WIDTH:RATE_COLS]], 0)


def taps_out(scratch, params, i, first, stride):
    rows_out(scratch, params[i, :, RATE_COLS:TAP_COLS], first, stride)
    at = first + stride * SUB
    scratch[at : at + CHUNKS, :] = params[i, 0:CHUNKS, TAP_COLS:PARAM_COLS]


def registers(scratch, count):
    return [scratch[j * SUB : (j + 1) * SUB, :] for j in range(count)]


def total(terms):
    while len(terms) > 1:
        terms = [x + y for x, y in zip(terms[::2], terms[1::2])]
    return terms[0]


def aligned(index):
    return pl.ds(pl.multiple_of(index, SUB), SUB)


def stage_body(branches, stride, feats, *refs):
    staged, done, held, sems = refs[-4:]
    rows, blocks = feats.shape[1], staged.shape[0]

    def fetch(i, b):
        column = pl.ds(i * WIDTH, WIDTH)
        return pltpu.make_async_copy(feats.at[branches[b], :, column], held.at[i, b], sems.at[i, b])

    for i in range(blocks):
        for b in range(len(branches)):
            fetch(i, b).start()
    for i in range(blocks):
        for b in range(len(branches)):
            fetch(i, b).wait()
            rows_out(staged.at[i], held[i, b].astype(F32), b * CHUNKS, stride)
    done[...] = jnp.zeros_like(done)


def pack_kernel(
    scale, filters_in, residues_in, rates_in, feats, wide, tail, filters, residues, rates, last, sems
):
    count = feats.shape[1]
    copies = [
        pltpu.make_async_copy(source, dest, sems.at[n])
        for n, (source, dest) in enumerate(
            (
                (rates_in, rates),
                (residues_in, residues),
                (filters_in, filters),
                (feats.at[:, count - SUB : count, :], last),
            )
        )
    ]
    for copy in copies:
        copy.start()
    copies[0].wait()
    copies[1].wait()
    for h in range(2):
        part = slice(h * HALF, (h + 1) * HALF)
        decayed = rates[part, :] * (2.0 * scale)
        power = jnp.tanh(0.5 * decayed) * (1.0 + jnp.exp(-decayed))
        wide[:, h * WIDTH : (h + 1) * WIDTH] = rates[part, :]
        at = PARAM_COLS + h * WIDTH
        wide[:, at : at + WIDTH] = residues[part, :] * jnp.sqrt(power)
    copies[2].wait()
    wide[:, TAP_COLS:PARAM_COLS] = jnp.zeros((SUB, LANES), F32)
    for r in range(TAPS):
        row = filters[r // 3, r % 3 : r % 3 + 1, :].astype(F32)
        if r < SUB:
            wide[r : r + 1, RATE_COLS:TAP_COLS] = row
        else:
            for k in range(CHUNKS):
                wide[k : k + 1, TAP_COLS:PARAM_COLS] = row[:, k * LANES : (k + 1) * LANES]
    copies[3].wait()
    for b in range(3):
        tail[b] = last[b, SUB - 2 : SUB, :]


def stack_kernel(*refs):
    params, coef = refs[-2:]
    for ref, i in zip(refs, NEAR + (0,)):
        params[i] = ref[:, 0:PARAM_COLS]
        for h in range(2):
            at = PARAM_COLS + h * WIDTH
            coef[i, h * HALF : (h + 1) * HALF, :] = ref[:, at : at + WIDTH]


def ends_kernel(
    scale, group, i, me, keyed, tail, params, ends, drive, last_s, taps_s, a_s, s_s
):
    rows = drive.shape[1] // SUB
    block = me[0] ^ (GROUP * i + group)
    column = pl.ds(pl.multiple_of(block * WIDTH, WIDTH), WIDTH)
    modes_out(a_s, jnp.exp(rates_of(params, i) * (-scale)))
    taps_out(taps_s, params, i, 0, CHUNKS)
    for branch, first in ((1, 0), (2, CHUNKS)):
        rows_out(last_s, tail[branch, :, column].astype(F32), first, SUB)
    a = registers(a_s, HALF)
    tap = [taps_s[pl.ds((3 * j + 1) * CHUNKS, SUB), :] for j in range(3)]

    def step(t0, carry):
        state, f1, f2 = carry
        state = list(state)
        for u in range(UNROLL):
            at = aligned((t0 * UNROLL + u) * SUB)
            f0 = keyed[block, at, :]
            filtered = tap[0] * f0 + tap[1] * f1 + tap[2] * f2
            now = filtered * pltpu.roll(filtered, CHUNKS, 0)
            drive[i, at, :] = now
            for j in range(HALF):
                state[j] = a[j] * state[j] + now
            f1, f2 = f0, f1
        return tuple(state), f1, f2

    start = ((jnp.zeros((SUB, LANES), F32),) * HALF, last_s[SUB : 2 * SUB, :], last_s[0:SUB, :])
    state = lax.fori_loop(0, rows // UNROLL, step, start)[0]
    for j in range(HALF):
        s_s[j * SUB : (j + 1) * SUB, :] = state[j]
    for h in range(2):
        for k in range(CHUNKS):
            ends[i, h * HALF : (h + 1) * HALF, k * LANES : (k + 1) * LANES] = s_s[
                pl.ds(h * CHUNKS + k, HALF, stride=SUB), :
            ]


def inner_kernel(
    scale, group, i, me, query, tail, params, coef, drive, packed, last_s, taps_s, a_s, c_s
):
    rows = drive.shape[1] // SUB
    block = me[0] ^ (GROUP * i + group)
    column = pl.ds(pl.multiple_of(block * WIDTH, WIDTH), WIDTH)
    modes_out(a_s, jnp.exp(rates_of(params, i) * (-scale)))
    modes_out(c_s, coef[i])
    for twice in range(2):
        taps_out(taps_s, params, i, twice * CHUNKS, SUB)
    rows_out(last_s, tail[0, :, column].astype(F32), 0, CHUNKS)
    a = registers(a_s, HALF)
    c = registers(c_s, HALF)
    tap = [taps_s[3 * j * SUB : (3 * j + 1) * SUB, :] for j in range(3)]
    upper = lax.broadcasted_iota(jnp.int32, (SUB, LANES), 0) >= CHUNKS

    def step(t0, carry):
        state, before = carry
        state = list(state)
        for u in range(0, UNROLL, 2):
            latest = query[block, aligned((t0 * UNROLL + u) * CHUNKS), :]
            middle = pltpu.roll(jnp.where(upper, before, latest), CHUNKS, 0)
            filtered = tap[0] * latest + tap[1] * middle + tap[2] * before
            before = latest
            for v, q in ((0, pltpu.roll(filtered, CHUNKS, 0)), (1, filtered)):
                at = aligned((t0 * UNROLL + u + v) * SUB)
                now = drive[i, at, :]
                for j in range(HALF):
                    state[j] = a[j] * state[j] + now
                y = total([x * s for x, s in zip(c, state)])
                packed[i, at, :] = jnp.where(upper, q, y + pltpu.roll(y, CHUNKS, 0))
        return tuple(state), before

    start = ((jnp.zeros((SUB, LANES), F32),) * HALF, last_s[0:SUB, :])
    lax.fori_loop(0, rows // UNROLL, step, start)


def finish_kernel(scale, i, params, packed, coef, incoming, held, a_s, p_s, y_s):
    rows = held.shape[1]
    decay = jnp.exp(rates_of(params, i) * (-scale))
    modes_out(a_s, decay)
    modes_out(p_s, coef[i] * decay * incoming[i])
    a = registers(a_s, HALF)

    def step(t0, p):
        p = list(p)
        for u in range(UNROLL):
            at = aligned((t0 * UNROLL + u) * SUB)
            z = packed[i, at, :]
            y = total(p)
            y = y + pltpu.roll(y, CHUNKS, 0)
            y_s[at, :] = (z + y) * pltpu.roll(z, CHUNKS, 0)
            p = [x * d for x, d in zip(p, a)]
        return tuple(p)

    lax.fori_loop(0, rows // UNROLL, step, tuple(registers(p_s, HALF)))
    for k in range(CHUNKS):
        held[i, :, k * LANES : (k + 1) * LANES] = y_s[pl.ds(k, rows, stride=SUB), :].astype(
            held.dtype
        )


def finish_body(scale, group, me, packed, params, coef, incoming, *refs):
    final = group == GROUPS - 1
    mine, a_s, p_s, y_s, sems = refs[-5:]
    out = refs[-6] if group else None

    def home(source, g, i, sem):
        column = pl.ds(pl.multiple_of((me[0] ^ (GROUP * i + g)) * WIDTH, WIDTH), WIDTH)
        return pltpu.make_async_copy(source.at[i], out.at[:, column], sems.at[sem, i])

    if group:
        for i in range(GROUP):
            home(refs[0], group - 1, i, 0).start()

    def one(i, carry):
        finish_kernel(scale, i, params, packed, coef, incoming, mine, a_s, p_s, y_s)
        if final:
            home(mine, group, i, 1).start()
        return carry

    lax.fori_loop(0, GROUP, one, 0)
    for i in range(GROUP):
        if group:
            home(refs[0], group - 1, i, 0).wait()
        if final:
            home(mine, group, i, 1).wait()


def pieces(kernel, skip, *refs):
    refs = refs[:1] + refs[1 + skip :]

    def one(i, carry):
        kernel(i, *refs)
        return carry

    lax.fori_loop(0, GROUP, one, 0)


def whole(inputs, outputs, scratch, more=(), smem=1, room=4):
    return dict(
        compiler_params=pltpu.CompilerParams(vmem_limit_bytes=room << 20),
        in_specs=[pl.BlockSpec(memory_space=pltpu.SMEM)] * smem + inputs,
        out_specs=outputs,
        scratch_shapes=[pltpu.VMEM((n, LANES), F32) for n in scratch] + list(more),
    )


def cost(rows, ops):
    work = GROUP * rows * SUB * LANES * ops
    return pl.CostEstimate(flops=work, bytes_accessed=work // 4, transcendentals=0)


ANYWHERE = pl.BlockSpec(memory_space=pl.ANY)


def stage_part(branches, feats, *earlier):
    rows, blocks = feats.shape[1], feats.shape[2] // WIDTH
    stride = CHUNKS * len(branches)
    return pl.pallas_call(
        functools.partial(stage_body, branches, stride),
        out_shape=(
            pltpu.VMEM((blocks, rows * stride, LANES), F32),
            pltpu.VMEM((SUB, LANES), F32),
        ),
        cost_estimate=cost(rows, 20 * len(branches)),
        name="stage_part",
        **whole(
            [HBM] + [ANYWHERE] * len(earlier),
            [VMEM] * 2,
            (),
            (
                pltpu.VMEM((blocks, len(branches), rows, WIDTH), feats.dtype),
                pltpu.SemaphoreType.DMA((blocks, len(branches))),
            ),
            smem=0,
            room=8,
        ),
    )(in_hbm(feats), *earlier)


def in_hbm(value):
    return pltpu.with_memory_space_constraint(value, pltpu.HBM)


def pack_part(filters, residues, rates, feats, scale):
    width = feats.shape[2]
    return pl.pallas_call(
        functools.partial(pack_kernel, scale),
        out_shape=(
            pltpu.VMEM((SUB, PARAM_COLS + 2 * WIDTH), F32),
            pltpu.VMEM((3, 2, width), feats.dtype),
        ),
        name="pack_part",
        **whole(
            [HBM] * 4,
            [VMEM] * 2,
            (),
            (
                pltpu.VMEM(filters.shape, filters.dtype),
                pltpu.VMEM((MODES, WIDTH), F32),
                pltpu.VMEM((MODES, WIDTH), F32),
                pltpu.VMEM((3, SUB, width), feats.dtype),
                pltpu.SemaphoreType.DMA((4,)),
            ),
            smem=0,
        ),
    )(in_hbm(filters), in_hbm(residues), in_hbm(rates), in_hbm(feats))


def stack_part(parts, *earlier):
    return pl.pallas_call(
        stack_kernel,
        out_shape=(
            pltpu.VMEM((GROUP, SUB, PARAM_COLS), F32),
            pltpu.VMEM((GROUP, MODES, WIDTH), F32),
        ),
        cost_estimate=pl.CostEstimate(flops=1 << 18, bytes_accessed=1 << 18, transcendentals=0),
        name="stack_part",
        **whole([VMEM] * GROUP + [ANYWHERE] * len(earlier), [VMEM] * 2, (), smem=0),
    )(*parts, *earlier)


def ends_part(group, me, keyed, tail, params, scale, *earlier):
    rows = keyed.shape[1] // SUB
    return pl.pallas_call(
        functools.partial(
            pieces, functools.partial(ends_kernel, scale, group), len(earlier)
        ),
        out_shape=(
            pltpu.VMEM((GROUP, MODES, WIDTH), F32),
            pltpu.VMEM((GROUP, rows * SUB, LANES), F32),
        ),
        cost_estimate=cost(rows, 24),
        name="ends_part",
        **whole(
            [ANYWHERE] * len(earlier) + [VMEM] * 3,
            [VMEM] * 2,
            (2 * SUB, TAPS * CHUNKS, HALF * SUB, HALF * SUB),
        ),
    )(me, *earlier, keyed, tail, params)


def inner_part(group, me, query, tail, params, coef, drive, scale):
    rows = drive.shape[1] // SUB
    return pl.pallas_call(
        functools.partial(pieces, functools.partial(inner_kernel, scale, group), 0),
        out_shape=pltpu.VMEM((GROUP, rows * SUB, LANES), F32),
        cost_estimate=cost(rows, 36),
        name="inner_part",
        **whole([VMEM] * 5, VMEM, (2 * CHUNKS, TAPS * SUB, HALF * SUB, HALF * SUB)),
    )(me, query, tail, params, coef, drive)


def finish_part(group, me, packed, params, coef, incoming, before, scale):
    rows, width = packed.shape[1] // SUB, GROUPS * GROUP * WIDTH
    final = group == GROUPS - 1
    held = (GROUP, rows, WIDTH)
    out_shape, out_specs, more = [], [], []
    if group:
        out_shape.append(jax.ShapeDtypeStruct((rows, width), jnp.bfloat16))
        out_specs.append(ANYWHERE)
    if final:
        more.append(pltpu.VMEM(held, jnp.bfloat16))
    else:
        out_shape.append(pltpu.VMEM(held, jnp.bfloat16))
        out_specs.append(VMEM)
    given_specs = [VMEM, ANYWHERE][: len(before)]
    spec = whole(
        [VMEM] * 4 + given_specs,
        out_specs,
        (),
        more
        + [pltpu.VMEM((n, LANES), F32) for n in (HALF * SUB, HALF * SUB, rows * SUB)]
        + [pltpu.SemaphoreType.DMA((2, GROUP))],
    )
    return pl.pallas_call(
        functools.partial(finish_body, scale, group),
        out_shape=out_shape,
        cost_estimate=cost(rows, 20),
        name="finish_part",
        input_output_aliases={6: 0} if len(before) > 1 else {},
        **spec,
    )(me, packed, params, coef, incoming, *before)


CORE, Y, Z = 1, 2, 4
NEAR = (3, 2, 1)


def swap(value, bit):
    size = lax.axis_size("ctx")
    return lax.ppermute(value, "ctx", [(i, i ^ bit) for i in range(size)])


def small(kernel, count, name, me, *args):
    return pl.pallas_call(
        kernel,
        out_shape=tuple(pltpu.VMEM((GROUP, MODES, WIDTH), F32) for _ in range(count)),
        cost_estimate=pl.CostEstimate(flops=1 << 18, bytes_accessed=1 << 18, transcendentals=0),
        name=name,
        **whole([VMEM] * len(args), [VMEM] * count, ()),
    )(me, *args)


def join_kernel(bit, span, flip, me, mine, theirs, params, low, both):
    later = (me[0] & bit) != 0
    for i in range(GROUP):
        m, t = mine[i], theirs[i ^ flip]
        decay = jnp.exp(rates_of(params, i) * (-span))
        first = jnp.where(later, t, m)
        low[i] = first
        both[i] = decay * first + jnp.where(later, m, t)


def turn_kernel(span, me, first, far, plane_low, core_low, params, row_out, mine, core_out):
    core, row = (me[0] & CORE) != 0, (me[0] & Y) != 0
    odd, high = (me[0] & Z) != 0, (me[0] & (2 * Z)) != 0
    for i in range(GROUP):
        rates = rates_of(params, i)
        reach = jnp.where(odd, jnp.exp(rates * (-4 * span)), 1.0)
        before = jnp.where(odd, first[i], 0.0) + jnp.where(high, reach * far[i ^ 2], 0.0)
        after = jnp.exp(rates * (-2 * span)) * before + plane_low[i]
        row_out[i] = jnp.where(row, before, after)
        before = jnp.where(row, after, before)
        after = jnp.exp(rates * (-span)) * before + core_low[i]
        core_out[i] = jnp.where(core, before, after)
        mine[i] = jnp.where(core, after, before)


def core_kernel(span, me, given, core_low, params, mine, core_out):
    core = (me[0] & CORE) != 0
    for i in range(GROUP):
        before = given[i]
        after = jnp.exp(rates_of(params, i) * (-span)) * before + core_low[i]
        core_out[i] = jnp.where(core, before, after)
        mine[i] = jnp.where(core, after, before)


def join(bit, span, flip, *args):
    return small(functools.partial(join_kernel, bit, span, flip), 2, "join", *args)


def after(value, *others):
    return lax.optimization_barrier((value,) + others)


def to_groups(value):
    pieces = value.reshape(value.shape[0], -1, WIDTH).transpose(1, 0, 2)
    return [pieces[g::GROUPS] for g in range(GROUPS)]


def by_owner(ends, rates_t, span):
    size = lax.axis_size("ctx")
    pieces = jnp.stack(ends, 1).reshape((-1,) + ends[0].shape[1:])
    blocks = pieces.transpose(1, 0, 2).reshape(MODES, size, -1).transpose(1, 0, 2)
    blocks = lax.all_to_all(blocks, "ctx", 0, 0, tiled=True)
    decay = jnp.exp(rates_t * (-span))

    def advance(carry, end):
        return decay * carry + end, carry

    before = lax.scan(advance, jnp.zeros_like(blocks[0]), blocks)[1]
    before = lax.all_to_all(before, "ctx", 0, 0, tiled=True)
    return to_groups(before.transpose(1, 0, 2).reshape(MODES, -1))


def by_gathers(feats, tail, short_filter, residues, rates, scale, span):
    rates_t = rates.T
    taps = short_filter.astype(F32).reshape(TAPS, -1)
    coef_t = (residues * jnp.sqrt(-jnp.expm1(-2.0 * rates * scale))).T
    named = jnp.concatenate([rates_t, taps, coef_t], 0)
    named = lax.all_gather(named, "ctx", axis=1, tiled=True)
    last = named[MODES + SUB].reshape(-1, CHUNKS, LANES)
    last = jnp.pad(last, ((0, 0), (0, SUB - CHUNKS), (0, 0)))
    named = named.reshape(named.shape[0], -1, WIDTH).transpose(1, 0, 2)
    parts = [named[:, k * SUB : (k + 1) * SUB] for k in range(3)]
    params = jnp.concatenate(parts + [last], 2)
    params = [params[g::GROUPS] for g in range(GROUPS)]
    coef = [named[g::GROUPS, MODES + TAPS :] for g in range(GROUPS)]
    base = jnp.zeros((1,), jnp.int32)
    keyed, query = stage_part((1, 2), feats)[0], stage_part((0,), feats)[0]
    groups = range(GROUPS)
    ends, drive = zip(*[ends_part(g, base, keyed, tail, params[g], scale) for g in groups])
    packed = [inner_part(g, base, query, tail, params[g], coef[g], drive[g], scale) for g in groups]
    incoming = by_owner(ends, rates_t, span)
    done = ()
    for g in groups:
        done = finish_part(g, base, packed[g], params[g], coef[g], incoming[g], done[::-1], scale)
    return done[0]


def per_device(features, short_filter, residues, rates):
    rows = features.shape[0]
    size = lax.axis_size("ctx")
    me = lax.axis_index("ctx").astype(jnp.int32)
    scale = 1.0 / (rows * size)
    feats = features.transpose(1, 0, 2)
    onward = [(i, i + 1) for i in range(size - 1)]
    span = rows * scale
    if rates.shape[0] != WIDTH or size != GROUP * GROUPS:
        tail = lax.ppermute(feats[:, -2:], "ctx", onward)
        return by_gathers(feats, tail, short_filter, residues, rates, scale, span)

    base = me.reshape(1)
    wide, tail_rows = pack_part(short_filter, residues.T, rates.T, feats, scale)
    near = [swap(wide, Z * k) for k in NEAR]
    tail = lax.ppermute(tail_rows, "ctx", onward)
    keyed, staged = stage_part((1, 2), feats, wide, base)
    query, staged = stage_part((0,), feats, staged)
    params, coef = ([x] for x in stack_part(near + [wide], staged, tail))
    params.append(swap(params[0], CORE))
    params.append(swap(params[0], Y))
    tail = lax.ppermute(tail_rows, "ctx", onward)
    coef.append(swap(coef[0], CORE))
    ends, drive, packed = [None] * GROUPS, [None] * GROUPS, [None] * GROUPS

    def run_ends(g, *earlier):
        ends[g], drive[g] = ends_part(g, base, keyed, tail, params[g], scale, *earlier)

    def run_inner(g):
        packed[g] = inner_part(g, base, query, tail, params[g], coef[g], drive[g], scale)

    run_ends(0)
    run_ends(1, ends[0])
    from_1 = swap(ends[1], CORE)
    params[2], ends[1] = after(params[2], ends[1])
    params.append(swap(params[2], CORE))
    run_ends(2)
    low_z, chip_z = join(CORE, span, 0, base, ends[0], from_1, params[0])
    params[3], ends[2] = after(params[3], ends[2])
    run_ends(3)
    from_3 = swap(ends[3], CORE)
    low_y, chip_y = join(CORE, span, 0, base, ends[2], from_3, params[2])
    from_y = swap(chip_y, Y)
    run_inner(0)
    from_y, packed[0], drive[1] = after(from_y, packed[0], drive[1])
    low, plane = join(Y, 2 * span, 0, base, chip_z, from_y, params[0])
    from_near = swap(plane, Z)
    coef.append(swap(coef[0], Y))
    run_inner(1)
    from_near, packed[1], coef[2] = after(from_near, packed[1], coef[2])
    first, pair = join(Z, 4 * span, 1, base, plane, from_near, params[0])
    from_far = swap(pair, 2 * Z)
    coef.append(swap(coef[2], CORE))
    run_inner(2)
    run_inner(3)
    from_far, packed[2], packed[3] = after(from_far, packed[2], packed[3])
    to_row, mine_z, to_core = small(
        functools.partial(turn_kernel, span),
        3,
        "turn",
        base,
        first,
        from_far,
        low,
        low_z,
        params[0],
    )
    from_row = swap(to_row, Y)
    core_z = swap(to_core, CORE)
    done = finish_part(0, base, packed[0], params[0], coef[0], mine_z, (), scale)
    done = finish_part(1, base, packed[1], params[1], coef[1], core_z, done[::-1], scale)
    from_row, held = after(from_row, done[1])
    mine_y, to_core = small(
        functools.partial(core_kernel, span), 2, "turn_core", base, from_row, low_y, params[2]
    )
    core_y = swap(to_core, CORE)
    done = finish_part(2, base, packed[2], params[2], coef[2], mine_y, (held, done[0]), scale)
    return finish_part(3, base, packed[3], params[3], coef[3], core_y, done[::-1], scale)[0]


def solution(mesh):
    in_specs = (
        P(("groups", "ctx"), None, None),
        P(None, None, "ctx"),
        P("ctx", None),
        P("ctx", None),
    )
    out_specs = P(("groups", "ctx"), None)
    return jax.shard_map(
        per_device, mesh=mesh, in_specs=in_specs, out_specs=out_specs, check_vma=False
    )
```

```python
import functools
import jax
import jax.numpy as jnp
from jax import lax
from jax.experimental import pallas as pl
from jax.experimental.pallas import tpu as pltpu
from jax.sharding import PartitionSpec as P

WIDTH = 512
LANES = 128
CHUNKS = WIDTH // LANES
HALF = 8
MODES = 2 * HALF
SUB = 8
TAPS = 9
RATE_COLS = 2 * WIDTH
TAP_COLS = RATE_COLS + WIDTH
PARAM_COLS = TAP_COLS + LANES
GROUP = 4
GROUPS = 4
UNROLL = 128
HBM = pl.BlockSpec(memory_space=pltpu.HBM)
F32 = jnp.float32
VMEM = pl.BlockSpec(memory_space=pltpu.VMEM)


def rows_out(scratch, natural, first, stride):
    for k in range(CHUNKS):
        scratch[pl.ds(first + k, natural.shape[0], stride=stride), :] = natural[
            :, k * LANES : (k + 1) * LANES
        ]


def modes_out(scratch, natural):
    for h in range(2):
        rows_out(scratch, natural[h * HALF : (h + 1) * HALF], h * CHUNKS, SUB)


def rates_of(params, i):
    return jnp.concatenate([params[i, :, 0:WIDTH], params[i, :, WIDTH:RATE_COLS]], 0)


def taps_out(scratch, params, i, first, stride):
    rows_out(scratch, params[i, :, RATE_COLS:TAP_COLS], first, stride)
    at = first + stride * SUB
    scratch[at : at + CHUNKS, :] = params[i, 0:CHUNKS, TAP_COLS:PARAM_COLS]


def registers(scratch, count):
    return [scratch[j * SUB : (j + 1) * SUB, :] for j in range(count)]


def total(terms):
    while len(terms) > 1:
        terms = [x + y for x, y in zip(terms[::2], terms[1::2])]
    return terms[0]


def aligned(index):
    return pl.ds(pl.multiple_of(index, SUB), SUB)


def stage_body(branches, stride, feats, *refs):
    staged, done, held, sems = refs[-4:]
    rows, blocks = feats.shape[1], staged.shape[0]

    def fetch(i, b):
        column = pl.ds(i * WIDTH, WIDTH)
        return pltpu.make_async_copy(feats.at[branches[b], :, column], held.at[i, b], sems.at[i, b])

    for i in range(blocks):
        for b in range(len(branches)):
            fetch(i, b).start()
    for i in range(blocks):
        for b in range(len(branches)):
            fetch(i, b).wait()
            rows_out(staged.at[i], held[i, b].astype(F32), b * CHUNKS, stride)
    done[...] = jnp.zeros_like(done)


def pack_kernel(scale, filters_in, residues_in, rates_in, wide, filters, residues, rates, sems):
    copies = [
        pltpu.make_async_copy(source, dest, sems.at[n])
        for n, (source, dest) in enumerate(
            ((rates_in, rates), (residues_in, residues), (filters_in, filters))
        )
    ]
    for copy in copies:
        copy.start()
    copies[0].wait()
    copies[1].wait()
    for h in range(2):
        part = slice(h * HALF, (h + 1) * HALF)
        decayed = rates[part, :] * (2.0 * scale)
        power = jnp.tanh(0.5 * decayed) * (1.0 + jnp.exp(-decayed))
        wide[:, h * WIDTH : (h + 1) * WIDTH] = rates[part, :]
        at = PARAM_COLS + h * WIDTH
        wide[:, at : at + WIDTH] = residues[part, :] * jnp.sqrt(power)
    copies[2].wait()
    wide[:, TAP_COLS:PARAM_COLS] = jnp.zeros((SUB, LANES), F32)
    for r in range(TAPS):
        row = filters[r // 3, r % 3 : r % 3 + 1, :].astype(F32)
        if r < SUB:
            wide[r : r + 1, RATE_COLS:TAP_COLS] = row
        else:
            for k in range(CHUNKS):
                wide[k : k + 1, TAP_COLS:PARAM_COLS] = row[:, k * LANES : (k + 1) * LANES]


def tail_kernel(feats, *refs):
    tail, last, sem = refs[-3:]
    rows = feats.shape[1]
    copy = pltpu.make_async_copy(feats.at[:, rows - SUB : rows, :], last, sem)
    copy.start()
    copy.wait()
    for b in range(3):
        tail[b] = last[b, SUB - 2 : SUB, :]


def stack_kernel(*refs):
    params, coef = refs[-2:]
    for ref, i in zip(refs, NEAR + (0,)):
        params[i] = ref[:, 0:PARAM_COLS]
        for h in range(2):
            at = PARAM_COLS + h * WIDTH
            coef[i, h * HALF : (h + 1) * HALF, :] = ref[:, at : at + WIDTH]


def ends_kernel(
    scale, group, i, me, keyed, tail, params, ends, drive, last_s, taps_s, a_s, s_s
):
    rows = drive.shape[1] // SUB
    block = me[0] ^ (GROUP * i + group)
    column = pl.ds(pl.multiple_of(block * WIDTH, WIDTH), WIDTH)
    modes_out(a_s, jnp.exp(rates_of(params, i) * (-scale)))
    taps_out(taps_s, params, i, 0, CHUNKS)
    for branch, first in ((1, 0), (2, CHUNKS)):
        rows_out(last_s, tail[branch, :, column].astype(F32), first, SUB)
    a = registers(a_s, HALF)
    tap = [taps_s[pl.ds((3 * j + 1) * CHUNKS, SUB), :] for j in range(3)]

    def step(t0, carry):
        state, f1, f2 = carry
        state = list(state)
        for u in range(UNROLL):
            at = aligned((t0 * UNROLL + u) * SUB)
            f0 = keyed[block, at, :]
            filtered = tap[0] * f0 + tap[1] * f1 + tap[2] * f2
            now = filtered * pltpu.roll(filtered, CHUNKS, 0)
            drive[i, at, :] = now
            for j in range(HALF):
                state[j] = a[j] * state[j] + now
            f1, f2 = f0, f1
        return tuple(state), f1, f2

    start = ((jnp.zeros((SUB, LANES), F32),) * HALF, last_s[SUB : 2 * SUB, :], last_s[0:SUB, :])
    state = lax.fori_loop(0, rows // UNROLL, step, start)[0]
    for j in range(HALF):
        s_s[j * SUB : (j + 1) * SUB, :] = state[j]
    for h in range(2):
        for k in range(CHUNKS):
            ends[i, h * HALF : (h + 1) * HALF, k * LANES : (k + 1) * LANES] = s_s[
                pl.ds(h * CHUNKS + k, HALF, stride=SUB), :
            ]


def inner_kernel(
    scale, group, i, me, query, tail, params, coef, drive, packed, last_s, taps_s, a_s, c_s
):
    rows = drive.shape[1] // SUB
    block = me[0] ^ (GROUP * i + group)
    column = pl.ds(pl.multiple_of(block * WIDTH, WIDTH), WIDTH)
    modes_out(a_s, jnp.exp(rates_of(params, i) * (-scale)))
    modes_out(c_s, coef[i])
    for twice in range(2):
        taps_out(taps_s, params, i, twice * CHUNKS, SUB)
    rows_out(last_s, tail[0, :, column].astype(F32), 0, CHUNKS)
    a = registers(a_s, HALF)
    c = registers(c_s, HALF)
    tap = [taps_s[3 * j * SUB : (3 * j + 1) * SUB, :] for j in range(3)]
    upper = lax.broadcasted_iota(jnp.int32, (SUB, LANES), 0) >= CHUNKS

    def step(t0, carry):
        state, before = carry
        state = list(state)
        for u in range(0, UNROLL, 2):
            latest = query[block, aligned((t0 * UNROLL + u) * CHUNKS), :]
            middle = pltpu.roll(jnp.where(upper, before, latest), CHUNKS, 0)
            filtered = tap[0] * latest + tap[1] * middle + tap[2] * before
            before = latest
            for v, q in ((0, pltpu.roll(filtered, CHUNKS, 0)), (1, filtered)):
                at = aligned((t0 * UNROLL + u + v) * SUB)
                now = drive[i, at, :]
                for j in range(HALF):
                    state[j] = a[j] * state[j] + now
                y = total([x * s for x, s in zip(c, state)])
                packed[i, at, :] = jnp.where(upper, q, y + pltpu.roll(y, CHUNKS, 0))
        return tuple(state), before

    start = ((jnp.zeros((SUB, LANES), F32),) * HALF, last_s[0:SUB, :])
    lax.fori_loop(0, rows // UNROLL, step, start)


def finish_kernel(scale, i, params, packed, coef, incoming, held, a_s, p_s, y_s):
    rows = held.shape[1]
    decay = jnp.exp(rates_of(params, i) * (-scale))
    modes_out(a_s, decay)
    modes_out(p_s, coef[i] * decay * incoming[i])
    a = registers(a_s, HALF)

    def step(t0, p):
        p = list(p)
        for u in range(UNROLL):
            at = aligned((t0 * UNROLL + u) * SUB)
            z = packed[i, at, :]
            y = total(p)
            y = y + pltpu.roll(y, CHUNKS, 0)
            y_s[at, :] = (z + y) * pltpu.roll(z, CHUNKS, 0)
            p = [x * d for x, d in zip(p, a)]
        return tuple(p)

    lax.fori_loop(0, rows // UNROLL, step, tuple(registers(p_s, HALF)))
    for k in range(CHUNKS):
        held[i, :, k * LANES : (k + 1) * LANES] = y_s[pl.ds(k, rows, stride=SUB), :].astype(
            held.dtype
        )


def finish_body(scale, group, me, packed, params, coef, incoming, *refs):
    final = group == GROUPS - 1
    mine, a_s, p_s, y_s, sems = refs[-5:]
    out = refs[-6] if group else None

    def home(source, g, i, sem):
        column = pl.ds(pl.multiple_of((me[0] ^ (GROUP * i + g)) * WIDTH, WIDTH), WIDTH)
        return pltpu.make_async_copy(source.at[i], out.at[:, column], sems.at[sem, i])

    if group:
        for i in range(GROUP):
            home(refs[0], group - 1, i, 0).start()

    def one(i, carry):
        finish_kernel(scale, i, params, packed, coef, incoming, mine, a_s, p_s, y_s)
        if final:
            home(mine, group, i, 1).start()
        return carry

    lax.fori_loop(0, GROUP, one, 0)
    for i in range(GROUP):
        if group:
            home(refs[0], group - 1, i, 0).wait()
        if final:
            home(mine, group, i, 1).wait()


def pieces(kernel, skip, *refs):
    refs = refs[:1] + refs[1 + skip :]

    def one(i, carry):
        kernel(i, *refs)
        return carry

    lax.fori_loop(0, GROUP, one, 0)


def whole(inputs, outputs, scratch, more=(), smem=1, room=4):
    return dict(
        compiler_params=pltpu.CompilerParams(vmem_limit_bytes=room << 20),
        in_specs=[pl.BlockSpec(memory_space=pltpu.SMEM)] * smem + inputs,
        out_specs=outputs,
        scratch_shapes=[pltpu.VMEM((n, LANES), F32) for n in scratch] + list(more),
    )


def cost(rows, ops):
    work = GROUP * rows * SUB * LANES * ops
    return pl.CostEstimate(flops=work, bytes_accessed=work // 4, transcendentals=0)


ANYWHERE = pl.BlockSpec(memory_space=pl.ANY)


def stage_part(branches, feats, *earlier):
    rows, blocks = feats.shape[1], feats.shape[2] // WIDTH
    stride = CHUNKS * len(branches)
    return pl.pallas_call(
        functools.partial(stage_body, branches, stride),
        out_shape=(
            pltpu.VMEM((blocks, rows * stride, LANES), F32),
            pltpu.VMEM((SUB, LANES), F32),
        ),
        cost_estimate=cost(rows, 20 * len(branches)),
        name="stage_part",
        **whole(
            [HBM] + [ANYWHERE] * len(earlier),
            [VMEM] * 2,
            (),
            (
                pltpu.VMEM((blocks, len(branches), rows, WIDTH), feats.dtype),
                pltpu.SemaphoreType.DMA((blocks, len(branches))),
            ),
            smem=0,
            room=8,
        ),
    )(in_hbm(feats), *earlier)


def in_hbm(value):
    return pltpu.with_memory_space_constraint(value, pltpu.HBM)


def pack_part(filters, residues, rates, scale):
    return pl.pallas_call(
        functools.partial(pack_kernel, scale),
        out_shape=pltpu.VMEM((SUB, PARAM_COLS + 2 * WIDTH), F32),
        name="pack_part",
        **whole(
            [HBM] * 3,
            VMEM,
            (),
            (
                pltpu.VMEM(filters.shape, filters.dtype),
                pltpu.VMEM((MODES, WIDTH), F32),
                pltpu.VMEM((MODES, WIDTH), F32),
                pltpu.SemaphoreType.DMA((3,)),
            ),
            smem=0,
        ),
    )(in_hbm(filters), in_hbm(residues), in_hbm(rates))


def tail_part(feats, *earlier):
    width = feats.shape[2]
    return pl.pallas_call(
        tail_kernel,
        out_shape=pltpu.VMEM((3, 2, width), feats.dtype),
        name="tail_part",
        **whole(
            [HBM] + [ANYWHERE] * len(earlier),
            VMEM,
            (),
            (pltpu.VMEM((3, SUB, width), feats.dtype), pltpu.SemaphoreType.DMA),
            smem=0,
        ),
    )(in_hbm(feats), *earlier)


def stack_part(parts, *earlier):
    return pl.pallas_call(
        stack_kernel,
        out_shape=(
            pltpu.VMEM((GROUP, SUB, PARAM_COLS), F32),
            pltpu.VMEM((GROUP, MODES, WIDTH), F32),
        ),
        cost_estimate=pl.CostEstimate(flops=1 << 18, bytes_accessed=1 << 18, transcendentals=0),
        name="stack_part",
        **whole([VMEM] * GROUP + [ANYWHERE] * len(earlier), [VMEM] * 2, (), smem=0),
    )(*parts, *earlier)


def ends_part(group, me, keyed, tail, params, scale, *earlier):
    rows = keyed.shape[1] // SUB
    return pl.pallas_call(
        functools.partial(
            pieces, functools.partial(ends_kernel, scale, group), len(earlier)
        ),
        out_shape=(
            pltpu.VMEM((GROUP, MODES, WIDTH), F32),
            pltpu.VMEM((GROUP, rows * SUB, LANES), F32),
        ),
        cost_estimate=cost(rows, 24),
        name="ends_part",
        **whole(
            [ANYWHERE] * len(earlier) + [VMEM] * 3,
            [VMEM] * 2,
            (2 * SUB, TAPS * CHUNKS, HALF * SUB, HALF * SUB),
        ),
    )(me, *earlier, keyed, tail, params)


def inner_part(group, me, query, tail, params, coef, drive, scale):
    rows = drive.shape[1] // SUB
    return pl.pallas_call(
        functools.partial(pieces, functools.partial(inner_kernel, scale, group), 0),
        out_shape=pltpu.VMEM((GROUP, rows * SUB, LANES), F32),
        cost_estimate=cost(rows, 36),
        name="inner_part",
        **whole([VMEM] * 5, VMEM, (2 * CHUNKS, TAPS * SUB, HALF * SUB, HALF * SUB)),
    )(me, query, tail, params, coef, drive)


def finish_part(group, me, packed, params, coef, incoming, before, scale):
    rows, width = packed.shape[1] // SUB, GROUPS * GROUP * WIDTH
    final = group == GROUPS - 1
    held = (GROUP, rows, WIDTH)
    out_shape, out_specs, more = [], [], []
    if group:
        out_shape.append(jax.ShapeDtypeStruct((rows, width), jnp.bfloat16))
        out_specs.append(ANYWHERE)
    if final:
        more.append(pltpu.VMEM(held, jnp.bfloat16))
    else:
        out_shape.append(pltpu.VMEM(held, jnp.bfloat16))
        out_specs.append(VMEM)
    given_specs = [VMEM, ANYWHERE][: len(before)]
    spec = whole(
        [VMEM] * 4 + given_specs,
        out_specs,
        (),
        more
        + [pltpu.VMEM((n, LANES), F32) for n in (HALF * SUB, HALF * SUB, rows * SUB)]
        + [pltpu.SemaphoreType.DMA((2, GROUP))],
    )
    return pl.pallas_call(
        functools.partial(finish_body, scale, group),
        out_shape=out_shape,
        cost_estimate=cost(rows, 20),
        name="finish_part",
        input_output_aliases={6: 0} if len(before) > 1 else {},
        **spec,
    )(me, packed, params, coef, incoming, *before)


CORE, Y, Z = 1, 2, 4
NEAR = (3, 2, 1)


def swap(value, bit):
    size = lax.axis_size("ctx")
    return lax.ppermute(value, "ctx", [(i, i ^ bit) for i in range(size)])


def small(kernel, count, name, me, *args):
    return pl.pallas_call(
        kernel,
        out_shape=tuple(pltpu.VMEM((GROUP, MODES, WIDTH), F32) for _ in range(count)),
        cost_estimate=pl.CostEstimate(flops=1 << 18, bytes_accessed=1 << 18, transcendentals=0),
        name=name,
        **whole([VMEM] * len(args), [VMEM] * count, ()),
    )(me, *args)


def join_kernel(bit, span, flip, me, mine, theirs, params, low, both):
    later = (me[0] & bit) != 0
    for i in range(GROUP):
        m, t = mine[i], theirs[i ^ flip]
        decay = jnp.exp(rates_of(params, i) * (-span))
        first = jnp.where(later, t, m)
        low[i] = first
        both[i] = decay * first + jnp.where(later, m, t)


def turn_kernel(span, me, first, far, plane_low, core_low, params, row_out, mine, core_out):
    core, row = (me[0] & CORE) != 0, (me[0] & Y) != 0
    odd, high = (me[0] & Z) != 0, (me[0] & (2 * Z)) != 0
    for i in range(GROUP):
        rates = rates_of(params, i)
        reach = jnp.where(odd, jnp.exp(rates * (-4 * span)), 1.0)
        before = jnp.where(odd, first[i], 0.0) + jnp.where(high, reach * far[i ^ 2], 0.0)
        after = jnp.exp(rates * (-2 * span)) * before + plane_low[i]
        row_out[i] = jnp.where(row, before, after)
        before = jnp.where(row, after, before)
        after = jnp.exp(rates * (-span)) * before + core_low[i]
        core_out[i] = jnp.where(core, before, after)
        mine[i] = jnp.where(core, after, before)


def core_kernel(span, me, given, core_low, params, mine, core_out):
    core = (me[0] & CORE) != 0
    for i in range(GROUP):
        before = given[i]
        after = jnp.exp(rates_of(params, i) * (-span)) * before + core_low[i]
        core_out[i] = jnp.where(core, before, after)
        mine[i] = jnp.where(core, after, before)


def join(bit, span, flip, *args):
    return small(functools.partial(join_kernel, bit, span, flip), 2, "join", *args)


def after(value, *others):
    return lax.optimization_barrier((value,) + others)


def to_groups(value):
    pieces = value.reshape(value.shape[0], -1, WIDTH).transpose(1, 0, 2)
    return [pieces[g::GROUPS] for g in range(GROUPS)]


def by_owner(ends, rates_t, span):
    size = lax.axis_size("ctx")
    pieces = jnp.stack(ends, 1).reshape((-1,) + ends[0].shape[1:])
    blocks = pieces.transpose(1, 0, 2).reshape(MODES, size, -1).transpose(1, 0, 2)
    blocks = lax.all_to_all(blocks, "ctx", 0, 0, tiled=True)
    decay = jnp.exp(rates_t * (-span))

    def advance(carry, end):
        return decay * carry + end, carry

    before = lax.scan(advance, jnp.zeros_like(blocks[0]), blocks)[1]
    before = lax.all_to_all(before, "ctx", 0, 0, tiled=True)
    return to_groups(before.transpose(1, 0, 2).reshape(MODES, -1))


def by_gathers(feats, tail, short_filter, residues, rates, scale, span):
    rates_t = rates.T
    taps = short_filter.astype(F32).reshape(TAPS, -1)
    coef_t = (residues * jnp.sqrt(-jnp.expm1(-2.0 * rates * scale))).T
    named = jnp.concatenate([rates_t, taps, coef_t], 0)
    named = lax.all_gather(named, "ctx", axis=1, tiled=True)
    last = named[MODES + SUB].reshape(-1, CHUNKS, LANES)
    last = jnp.pad(last, ((0, 0), (0, SUB - CHUNKS), (0, 0)))
    named = named.reshape(named.shape[0], -1, WIDTH).transpose(1, 0, 2)
    parts = [named[:, k * SUB : (k + 1) * SUB] for k in range(3)]
    params = jnp.concatenate(parts + [last], 2)
    params = [params[g::GROUPS] for g in range(GROUPS)]
    coef = [named[g::GROUPS, MODES + TAPS :] for g in range(GROUPS)]
    base = jnp.zeros((1,), jnp.int32)
    keyed, query = stage_part((1, 2), feats)[0], stage_part((0,), feats)[0]
    groups = range(GROUPS)
    ends, drive = zip(*[ends_part(g, base, keyed, tail, params[g], scale) for g in groups])
    packed = [inner_part(g, base, query, tail, params[g], coef[g], drive[g], scale) for g in groups]
    incoming = by_owner(ends, rates_t, span)
    done = ()
    for g in groups:
        done = finish_part(g, base, packed[g], params[g], coef[g], incoming[g], done[::-1], scale)
    return done[0]


def per_device(features, short_filter, residues, rates):
    rows = features.shape[0]
    size = lax.axis_size("ctx")
    me = lax.axis_index("ctx").astype(jnp.int32)
    scale = 1.0 / (rows * size)
    feats = features.transpose(1, 0, 2)
    onward = [(i, i + 1) for i in range(size - 1)]
    span = rows * scale
    if rates.shape[0] != WIDTH or size != GROUP * GROUPS:
        tail = lax.ppermute(feats[:, -2:], "ctx", onward)
        return by_gathers(feats, tail, short_filter, residues, rates, scale, span)

    base = me.reshape(1)
    wide = pack_part(short_filter, residues.T, rates.T, scale)
    near = [swap(wide, Z * k) for k in NEAR]
    keyed, staged = stage_part((1, 2), feats, wide, base)
    tail_rows = tail_part(feats, staged)
    query, staged = stage_part((0,), feats, tail_rows)
    params, coef = ([x] for x in stack_part(near + [wide], tail_rows, staged))
    params.append(swap(params[0], CORE))
    params.append(swap(params[0], Y))
    tail = lax.ppermute(tail_rows, "ctx", onward)
    coef.append(swap(coef[0], CORE))
    ends, drive, packed = [None] * GROUPS, [None] * GROUPS, [None] * GROUPS

    def run_ends(g, *earlier):
        ends[g], drive[g] = ends_part(g, base, keyed, tail, params[g], scale, *earlier)

    def run_inner(g):
        packed[g] = inner_part(g, base, query, tail, params[g], coef[g], drive[g], scale)

    run_ends(0)
    run_ends(1, ends[0])
    from_1 = swap(ends[1], CORE)
    params[2], ends[1] = after(params[2], ends[1])
    params.append(swap(params[2], CORE))
    run_ends(2)
    low_z, chip_z = join(CORE, span, 0, base, ends[0], from_1, params[0])
    params[3], ends[2] = after(params[3], ends[2])
    run_ends(3)
    from_3 = swap(ends[3], CORE)
    low_y, chip_y = join(CORE, span, 0, base, ends[2], from_3, params[2])
    from_y = swap(chip_y, Y)
    run_inner(0)
    from_y, packed[0], drive[1] = after(from_y, packed[0], drive[1])
    low, plane = join(Y, 2 * span, 0, base, chip_z, from_y, params[0])
    from_near = swap(plane, Z)
    coef.append(swap(coef[0], Y))
    run_inner(1)
    from_near, packed[1], coef[2] = after(from_near, packed[1], coef[2])
    first, pair = join(Z, 4 * span, 1, base, plane, from_near, params[0])
    from_far = swap(pair, 2 * Z)
    coef.append(swap(coef[2], CORE))
    run_inner(2)
    run_inner(3)
    from_far, packed[2], packed[3] = after(from_far, packed[2], packed[3])
    to_row, mine_z, to_core = small(
        functools.partial(turn_kernel, span),
        3,
        "turn",
        base,
        first,
        from_far,
        low,
        low_z,
        params[0],
    )
    from_row = swap(to_row, Y)
    core_z = swap(to_core, CORE)
    done = finish_part(0, base, packed[0], params[0], coef[0], mine_z, (), scale)
    done = finish_part(1, base, packed[1], params[1], coef[1], core_z, done[::-1], scale)
    from_row, held = after(from_row, done[1])
    mine_y, to_core = small(
        functools.partial(core_kernel, span), 2, "turn_core", base, from_row, low_y, params[2]
    )
    core_y = swap(to_core, CORE)
    done = finish_part(2, base, packed[2], params[2], coef[2], mine_y, (held, done[0]), scale)
    return finish_part(3, base, packed[3], params[3], coef[3], core_y, done[::-1], scale)[0]


def solution(mesh):
    in_specs = (
        P(("groups", "ctx"), None, None),
        P(None, None, "ctx"),
        P("ctx", None),
        P("ctx", None),
    )
    out_specs = P(("groups", "ctx"), None)
    return jax.shard_map(
        per_device, mesh=mesh, in_specs=in_specs, out_specs=out_specs, check_vma=False
    )
```
